32 devices in a mesh: dp: 16 (over z, x, core), fsdp: 2 (over y).
Axes of the slice: x: 2, y: 2, z: 4, core: 2. Of those that a mesh axis runs over, the one named last changes fastest.
Arguments:
- inputs: float32 [96, 197, 384], P(('dp', 'fsdp')), may hold values from -6 to 6
- ln1_gain: float32 [384], P('fsdp'), may hold values from 0.5 to 2
- ln1_shift: float32 [384], P('fsdp'), may hold values from -3 to 3
- w_qkv: float32 [384, 1152], P('fsdp'), may hold values from -0.3125 to 0.3125
- q_bias: float32 [384], P('fsdp'), may hold values from -3 to 3
- v_bias: float32 [384], P('fsdp'), may hold values from -3 to 3
- w_proj: float32 [384, 384], P('fsdp'), may hold values from -0.875 to 0.875
- proj_bias: float32 [384], P('fsdp'), may hold values from -3 to 3
- ln2_gain: float32 [384], P('fsdp'), may hold values from 0.5 to 2
- ln2_shift: float32 [384], P('fsdp'), may hold values from -3 to 3
- w_fc1: float32 [384, 1536], P('fsdp'), may hold values from -0.3125 to 0.3125
- fc1_bias: float32 [1536], P('fsdp'), may hold values from -3 to 3
- w_fc2: float32 [1536, 384], P('fsdp'), may hold values from -0.21875 to 0.21875
- fc2_bias: float32 [384], P('fsdp'), may hold values from -3 to 3
- grad_output: float32 [96, 197, 384], P(('dp', 'fsdp')), may hold values from -6 to 6
Outputs:
- output: float32 [96, 197, 384], P(('dp', 'fsdp'))
- grad_inputs: float32 [96, 197, 384], P(('dp', 'fsdp'))
- grad_ln1_gain: float32 [384], P('fsdp')
- grad_ln1_shift: float32 [384], P('fsdp')
- grad_w_qkv: float32 [384, 1152], P('fsdp')
- grad_q_bias: float32 [384], P('fsdp')
- grad_v_bias: float32 [384], P('fsdp')
- grad_w_proj: float32 [384, 384], P('fsdp')
- grad_proj_bias: float32 [384], P('fsdp')
- grad_ln2_gain: float32 [384], P('fsdp')
- grad_ln2_shift: float32 [384], P('fsdp')
- grad_w_fc1: float32 [384, 1536], P('fsdp')
- grad_fc1_bias: float32 [1536], P('fsdp')
- grad_w_fc2: float32 [1536, 384], P('fsdp')
- grad_fc2_bias: float32 [384], P('fsdp')
The draws below stay inside these ranges and needn't reach their ends.
All inputs are finite; a program needn't handle non-finite values.
Results may differ from the reference program's by a relative error of at most 0.00026.
Values sent between devices are 32-bit elements; how exact they have to be, the bound alone decides.
No kernel may reach another device: no remote copies, remote signals or barrier semaphores. Data moves between devices by JAX's collectives and lax.ppermute only.
A program may use at most 128 MiB of HBM per device.

```python
import math
import jax
import jax.numpy as jnp
from jax import lax

D = 384
HEADS = 6
HEAD_DIM = 64
FF = 1536
SEQ = 197
IMG_DEV = 3
IMAGES = 96
N_FSDP = 2


def level_of(rng, shape, shards, smallest, largest):
    factor_of, own = 1.0, jax.random.fold_in(rng, 6)
    for axis_at, parts in shards:
        draws = jnp.exp(jax.random.uniform(jax.random.fold_in(own, axis_at), (parts,), jnp.float32, smallest / len(shards), largest / len(shards)))
        factor_of = factor_of * jnp.repeat(draws, shape[axis_at] // parts).reshape([-1 if axis == axis_at else 1 for axis in range(len(shape))])
    return factor_of


def normal_values(rng, dims, scale, most, cuts=(), held_as=jnp.bfloat16):
    loudness = level_of(rng, dims, cuts, -0.22, 0.18) if cuts else 1.0
    values = jax.random.normal(rng, dims, jnp.float32) * scale * loudness
    return jnp.minimum(jnp.maximum(values, -most), most).astype(held_as)


def setup_inputs(seed: int = 0) -> dict:
    streams_of = jax.random.split(jax.random.key(seed), 16)
    inputs = normal_values(streams_of[0], (IMAGES, SEQ, D), 1.0, 6.0, ((0, 32),), jnp.float32)
    ln1_gain = jnp.clip(jnp.exp(math.log(2.0) - 1.3862944 * jax.random.uniform(streams_of[1], (D,), jnp.float32) ** level_of(streams_of[1], (D,), ((0, 2),), -0.2, 0.2)), 0.5, 2.0)
    ln1_shift = normal_values(streams_of[2], (D,), 0.5, 3.0, ((0, 2),), jnp.float32)
    w_qkv = normal_values(streams_of[3], (D, 3 * D), D ** -0.5, 0.3125, ((0, 2),), jnp.float32)
    q_bias = normal_values(streams_of[4], (D,), 0.5, 3.0, ((0, 2),), jnp.float32)
    v_bias = normal_values(streams_of[5], (D,), 0.5, 3.0, ((0, 2),), jnp.float32)
    w_proj = normal_values(streams_of[6], (D, D), (D // 8) ** -0.5, 0.875, ((0, 2),), jnp.float32)
    proj_bias = normal_values(streams_of[7], (D,), 0.5, 3.0, ((0, 2),), jnp.float32)
    ln2_gain = jnp.clip(jnp.exp(math.log(2.0) - 1.3862944 * jax.random.uniform(streams_of[8], (D,), jnp.float32) ** level_of(streams_of[8], (D,), ((0, 2),), -0.2, 0.2)), 0.5, 2.0)
    ln2_shift = normal_values(streams_of[9], (D,), 0.5, 3.0, ((0, 2),), jnp.float32)
    w_fc1 = normal_values(streams_of[10], (D, FF), D ** -0.5, 0.3125, ((0, 2),), jnp.float32)
    fc1_bias = normal_values(streams_of[11], (FF,), 0.5, 3.0, ((0, 2),), jnp.float32)
    w_fc2 = normal_values(streams_of[12], (FF, D), (FF // 2) ** -0.5, 0.21875, ((0, 2),), jnp.float32)
    fc2_bias = normal_values(streams_of[13], (D,), 0.5, 3.0, ((0, 2),), jnp.float32)
    grad_output = normal_values(streams_of[14], (IMAGES, SEQ, D), 1.0, 6.0, ((0, 32),), jnp.float32)
    return dict(inputs=inputs, ln1_gain=ln1_gain, ln1_shift=ln1_shift, w_qkv=w_qkv, q_bias=q_bias, v_bias=v_bias, w_proj=w_proj, proj_bias=proj_bias, ln2_gain=ln2_gain, ln2_shift=ln2_shift, w_fc1=w_fc1, fc1_bias=fc1_bias, w_fc2=w_fc2, fc2_bias=fc2_bias, grad_output=grad_output)


EPS = 1e-06
HIGH = lax.Precision.HIGHEST

def dense_nn(left, right):
    return jnp.dot(left, right, precision=HIGH, preferred_element_type=jnp.float32)

def dense_tn(left, right):
    return lax.dot_general(left, right, (((0,), (0,)), ((), ())), precision=HIGH, preferred_element_type=jnp.float32)

def dense_nt(left, right):
    return lax.dot_general(left, right, (((1,), (1,)), ((), ())), precision=HIGH, preferred_element_type=jnp.float32)

def layer_norm(values, gain_vec, shift_vec):
    center = values - lax.optimization_barrier(jnp.mean(values, axis=-1, keepdims=True))
    inv_std = lax.rsqrt(lax.optimization_barrier(jnp.mean(center * center, axis=-1, keepdims=True)) + EPS)
    normed = center * inv_std
    return (normed * gain_vec + shift_vec, normed, inv_std)

def norm_back(grad_out, normed, inv_std, gain_vec):
    scaled = grad_out * gain_vec
    return inv_std * (scaled - lax.optimization_barrier(jnp.mean(scaled, axis=-1, keepdims=True)) - normed * lax.optimization_barrier(jnp.mean(scaled * normed, axis=-1, keepdims=True)))

def gelu_exact(values):
    return 0.5 * values * (1.0 + jax.scipy.special.erf(values / math.sqrt(2.0)))

def gelu_slope(values):
    return 0.5 * (1.0 + jax.scipy.special.erf(values / math.sqrt(2.0))) + values * jnp.exp(-0.5 * values * values) / math.sqrt(2.0 * math.pi)

def attend(queries, keys_all, values_all):
    scale = 1.0 / math.sqrt(HEAD_DIM)
    scores = jnp.einsum('bqhe,bkhe->bhqk', queries, keys_all, precision=HIGH) * scale
    top = lax.optimization_barrier(jnp.max(scores, axis=-1, keepdims=True))
    log_total = top + jnp.log(lax.optimization_barrier(jnp.sum(jnp.exp(scores - top), axis=-1, keepdims=True)))
    probs = jnp.exp(scores - log_total)
    context = jnp.einsum('bhqk,bkhe->bqhe', probs, values_all, precision=HIGH)
    return (context, log_total)

def attend_back(grad_ctx, queries, keys_all, values_all, context, log_total):
    scale = 1.0 / math.sqrt(HEAD_DIM)
    scores = jnp.einsum('bqhe,bkhe->bhqk', queries, keys_all, precision=HIGH) * scale
    probs = jnp.exp(scores - log_total)
    grad_probs = jnp.einsum('bqhe,bkhe->bhqk', grad_ctx, values_all, precision=HIGH)
    grad_values = jnp.einsum('bhqk,bqhe->bkhe', probs, grad_ctx, precision=HIGH)
    delta = jnp.transpose(lax.optimization_barrier(jnp.sum(grad_ctx * context, axis=-1)), (0, 2, 1))[..., None]
    grad_scores = probs * (grad_probs - delta)
    grad_queries = jnp.einsum('bhqk,bkhe->bqhe', grad_scores, keys_all, precision=HIGH) * scale
    grad_keys = jnp.einsum('bhqk,bqhe->bkhe', grad_scores, queries, precision=HIGH) * scale
    return (grad_queries, grad_keys, grad_values)

def layer_forward(inputs, params):
    ln1_gain, ln1_shift, w_qkv, q_bias, v_bias, w_proj, proj_bias, ln2_gain, ln2_shift, w_fc1, fc1_bias, w_fc2, fc2_bias = params
    batch = inputs.shape[0]
    flat_rows = inputs.reshape(-1, D)
    norm1_out, normed1, inv_std1 = layer_norm(flat_rows, ln1_gain, ln1_shift)
    joined = dense_nn(norm1_out, w_qkv)
    queries = (joined[:, :D] + q_bias).reshape(batch, SEQ, HEADS, HEAD_DIM)
    keys_all = joined[:, D:2 * D].reshape(batch, SEQ, HEADS, HEAD_DIM)
    values_all = (joined[:, 2 * D:] + v_bias).reshape(batch, SEQ, HEADS, HEAD_DIM)
    context, log_total = attend(queries, keys_all, values_all)
    ctx_rows = context.reshape(-1, D)
    middle = flat_rows + dense_nn(ctx_rows, w_proj) + proj_bias
    norm2_out, normed2, inv_std2 = layer_norm(middle, ln2_gain, ln2_shift)
    hidden_pre = dense_nn(norm2_out, w_fc1) + fc1_bias
    hidden_act = gelu_exact(hidden_pre)
    output = middle + dense_nn(hidden_act, w_fc2) + fc2_bias
    saved = (norm1_out, normed1, inv_std1, queries, keys_all, values_all, context, log_total, norm2_out, normed2, inv_std2, hidden_pre, hidden_act)
    return (output.reshape(inputs.shape), saved)

def layer_backward(grad_output, saved, params):
    ln1_gain, ln1_shift, w_qkv, q_bias, v_bias, w_proj, proj_bias, ln2_gain, ln2_shift, w_fc1, fc1_bias, w_fc2, fc2_bias = params
    norm1_out, normed1, inv_std1, queries, keys_all, values_all, context, log_total, norm2_out, normed2, inv_std2, hidden_pre, hidden_act = saved
    batch = grad_output.shape[0]
    grad_rows = grad_output.reshape(-1, D)
    grad_fc2 = dense_tn(hidden_act, grad_rows)
    grad_fc2_bias = lax.optimization_barrier(jnp.sum(grad_rows, axis=0))
    grad_pre = dense_nt(grad_rows, w_fc2) * gelu_slope(hidden_pre)
    grad_fc1 = dense_tn(norm2_out, grad_pre)
    grad_fc1_bias = lax.optimization_barrier(jnp.sum(grad_pre, axis=0))
    grad_norm2 = dense_nt(grad_pre, w_fc1)
    grad_gain2 = lax.optimization_barrier(jnp.sum(grad_norm2 * normed2, axis=0))
    grad_shift2 = lax.optimization_barrier(jnp.sum(grad_norm2, axis=0))
    grad_middle = grad_rows + norm_back(grad_norm2, normed2, inv_std2, ln2_gain)
    ctx_rows = context.reshape(-1, D)
    grad_proj = dense_tn(ctx_rows, grad_middle)
    grad_proj_bias = lax.optimization_barrier(jnp.sum(grad_middle, axis=0))
    grad_ctx = dense_nt(grad_middle, w_proj).reshape(batch, SEQ, HEADS, HEAD_DIM)
    grad_queries, grad_keys, grad_values = attend_back(grad_ctx, queries, keys_all, values_all, context, log_total)
    grad_joined = jnp.concatenate([grad_queries.reshape(-1, D), grad_keys.reshape(-1, D), grad_values.reshape(-1, D)], axis=1)
    grad_qkv = dense_tn(norm1_out, grad_joined)
    grad_qbias = lax.optimization_barrier(jnp.sum(grad_joined[:, :D], axis=0))
    grad_vbias = lax.optimization_barrier(jnp.sum(grad_joined[:, 2 * D:], axis=0))
    grad_norm1 = dense_nt(grad_joined, w_qkv)
    grad_gain1 = lax.optimization_barrier(jnp.sum(grad_norm1 * normed1, axis=0))
    grad_shift1 = lax.optimization_barrier(jnp.sum(grad_norm1, axis=0))
    grad_inputs = grad_middle + norm_back(grad_norm1, normed1, inv_std1, ln1_gain)
    grads = (grad_gain1, grad_shift1, grad_qkv, grad_qbias, grad_vbias, grad_proj, grad_proj_bias, grad_gain2, grad_shift2, grad_fc1, grad_fc1_bias, grad_fc2, grad_fc2_bias)
    return (grad_inputs.reshape(grad_output.shape), grads)

def reference(inputs, ln1_gain, ln1_shift, w_qkv, q_bias, v_bias, w_proj, proj_bias, ln2_gain, ln2_shift, w_fc1, fc1_bias, w_fc2, fc2_bias, grad_output):
    params = (ln1_gain, ln1_shift, w_qkv, q_bias, v_bias, w_proj, proj_bias, ln2_gain, ln2_shift, w_fc1, fc1_bias, w_fc2, fc2_bias)
    block_size = IMG_DEV * N_FSDP
    count = IMAGES // block_size
    input_blocks = inputs.reshape(count, block_size, SEQ, D)
    grad_blocks = grad_output.reshape(count, block_size, SEQ, D)

    def one_block(totals, pair):
        block_in, block_grad = pair
        block_out, saved = layer_forward(block_in, params)
        block_dx, grads = layer_backward(block_grad, saved, params)
        totals = tuple((total + grad for total, grad in zip(totals, grads)))
        return (totals, (block_out, block_dx))
    start = tuple((jnp.zeros(param.shape, jnp.float32) for param in params))
    totals, (outputs, grad_inputs) = lax.scan(one_block, start, (input_blocks, grad_blocks))
    return (outputs.reshape(IMAGES, SEQ, D), grad_inputs.reshape(IMAGES, SEQ, D)) + totals
```

```python
import math

import jax
import jax.numpy as jnp
from jax import lax
from jax.experimental import pallas as pl
from jax.experimental.pallas import tpu as pltpu
from jax.sharding import PartitionSpec as P

HEAD_DIM = 64
LANES = 128
EPS = 1e-06
F32 = jnp.float32
BF16 = jnp.bfloat16
VMEM_LIMIT = 56 * 1024 * 1024


def split(v):
    hi = v.astype(BF16)
    lo = (v - hi.astype(F32)).astype(BF16)
    return hi, lo


def dot(a, b, ca, cb):
    return lax.dot_general(a, b, (((ca,), (cb,)), ((), ())), preferred_element_type=F32)


def dot3(a, b, ca, cb):
    ah, al = a
    bh, bl = b
    return dot(ah, bh, ca, cb) + (dot(ah, bl, ca, cb) + dot(al, bh, ca, cb))


def row_sum(v):
    return jnp.sum(v, axis=0, keepdims=True)


def norm_parts(v):
    center = v - jnp.mean(v, axis=-1, keepdims=True)
    inv = lax.rsqrt(jnp.mean(center * center, axis=-1, keepdims=True) + EPS)
    return center * inv, inv


def norm_back(dh, n, inv, gain):
    s = dh * gain
    return inv * (
        s - jnp.mean(s, axis=-1, keepdims=True) - n * jnp.mean(s * n, axis=-1, keepdims=True)
    )


def load_weight(offs, k, pieces, hi_ref, lo_ref):
    for p in pieces:
        at = pl.multiple_of(offs[k], 16)
        hi, lo = split(p[...])
        hi_ref[pl.ds(at, p.shape[0]), :] = hi
        lo_ref[pl.ds(at, p.shape[0]), :] = lo
        k += 1
    return k


def both(hi_ref, lo_ref):
    return hi_ref[...], lo_ref[...]


def lane_lt(shape):
    return lax.broadcasted_iota(jnp.int32, shape, 1) < HEAD_DIM


def swap(v):
    return pltpu.roll(v, HEAD_DIM, 1)


def pair_left(v, low):
    hi = v.astype(BF16).astype(F32)
    lo = v - hi
    zero = jnp.zeros_like(v)
    h0 = jnp.concatenate([jnp.where(low, hi, swap(lo)), jnp.where(low, hi, zero)], axis=1)
    h1 = jnp.concatenate([jnp.where(low, swap(lo), hi), jnp.where(low, zero, hi)], axis=1)
    return h0.astype(BF16), h1.astype(BF16)


def pair_right(v, low):
    hi = v.astype(BF16).astype(F32)
    lo = v - hi
    rolled = swap(hi)
    h0 = jnp.concatenate([jnp.where(low, hi, rolled), lo], axis=1)
    h1 = jnp.concatenate([jnp.where(low, rolled, hi), lo], axis=1)
    return h0.astype(BF16), h1.astype(BF16)


def wide(v):
    hi, lo = split(v)
    return hi, jnp.concatenate([hi, lo], axis=1)


def dot_wide(ph, pl_, w, ca):
    hi, cat = w
    t = dot(ph, cat, ca, 0)
    return t[:, :LANES] + (t[:, LANES:] + dot(pl_, hi, ca, 0))


def part_rows(g_ref, send_ref, keep_ref, core):
    n, rows, _ = keep_ref.shape
    for i in range(n):
        at = pl.multiple_of(2 * i * rows + (1 - core) * rows, 8)
        send_ref[i] = g_ref[pl.ds(at, rows), :]
        at = pl.multiple_of(2 * i * rows + core * rows, 8)
        keep_ref[i] = g_ref[pl.ds(at, rows), :]


def part_cols(g_ref, send_ref, keep_ref, core):
    n, rows, cols = keep_ref.shape
    for i in range(n):
        at = pl.multiple_of((1 - core) * cols, LANES)
        send_ref[i] = g_ref[i * rows : (i + 1) * rows, pl.ds(at, cols)]
        at = pl.multiple_of(core * cols, LANES)
        keep_ref[i] = g_ref[i * rows : (i + 1) * rows, pl.ds(at, cols)]


def attn_fwd_kernel(np_, offs, x_ref, vec_ref, *refs):
    w_pieces = refs[:np_]
    qkv_ref, ctx_ref, ph_ref, pl_ref, wh, wl = refs[np_:]

    @pl.when(pl.program_id(0) == 0)
    def _():
        load_weight(offs, 0, w_pieces, wh, wl)

    d = x_ref.shape[2]
    vec = vec_ref[...]
    n1, _ = norm_parts(x_ref[0])
    h1 = n1 * vec[0:1] + vec[1:2]
    qkv = dot3(split(h1), both(wh, wl), 1, 0)
    q = qkv[:, :d] + vec[2:3]
    k = qkv[:, d : 2 * d]
    v = qkv[:, 2 * d :] + vec[3:4]
    qkv_ref[0, :, :d] = q
    qkv_ref[0, :, d : 2 * d] = k
    qkv_ref[0, :, 2 * d :] = v
    q = q * (1.0 / math.sqrt(HEAD_DIM))
    low = lane_lt((x_ref.shape[1], LANES))
    for j in range(d // LANES):
        sl = slice(j * LANES, (j + 1) * LANES)
        qs = pair_left(q[:, sl], low)
        ks = pair_right(k[:, sl], low)
        vw = wide(v[:, sl])
        outs = []
        for i in range(2):
            s = dot(qs[i], ks[i], 1, 1)
            e = jnp.exp(s - jnp.max(s, axis=-1, keepdims=True))
            p = e * (1.0 / jnp.sum(e, axis=-1, keepdims=True))
            hi, lo = split(p)
            ph_ref[0, 2 * j + i] = hi
            pl_ref[0, 2 * j + i] = lo
            outs.append(dot_wide(hi, lo, vw, 1))
        ctx_ref[0, :, sl] = jnp.where(low, outs[0], outs[1])


def mlp_fwd_kernel(na, nb, nc, offs, x_ref, ctx_ref, dy_ref, vec_ref, b1_ref, *refs):
    wp, w1, w2 = refs[:na], refs[na : na + nb], refs[na + nb : na + nb + nc]
    refs = refs[na + nb + nc :]
    out_ref, pre_ref, mid_ref, send_ref, keep_ref, gb2_ref = refs[:6]
    wph, wpl, w1h, w1l, w2h, w2l, g2_ref = refs[6:]
    first = pl.program_id(0) == 0

    @pl.when(first)
    def _():
        k = load_weight(offs, 0, wp, wph, wpl)
        k = load_weight(offs, k, w1, w1h, w1l)
        load_weight(offs, k, w2, w2h, w2l)
        g2_ref[...] = jnp.zeros_like(g2_ref)
        gb2_ref[...] = jnp.zeros_like(gb2_ref)

    vec = vec_ref[...]
    mid = x_ref[0] + dot3(split(ctx_ref[0]), both(wph, wpl), 1, 0) + vec[4:5]
    mid_ref[0] = mid
    n2, _ = norm_parts(mid)
    h2 = n2 * vec[5:6] + vec[6:7]
    pre = dot3(split(h2), both(w1h, w1l), 1, 0) + b1_ref[...]
    pre_ref[0] = pre
    act = 0.5 * pre * (1.0 + lax.erf(pre * (1.0 / math.sqrt(2.0))))
    act = split(act)
    out_ref[0] = mid + dot3(act, both(w2h, w2l), 1, 0) + vec[7:8]
    dy = dy_ref[0]
    g2_ref[...] += dot3(act, split(dy), 0, 0)
    gb2_ref[...] += row_sum(dy)

    @pl.when(pl.program_id(0) == pl.num_programs(0) - 1)
    def _():
        part_rows(g2_ref, send_ref, keep_ref, offs[na + nb + nc])


def mlp_bwd_kernel(na, nb, nc, offs, ctx_ref, dy_ref, pre_ref, mid_ref, vec_ref, *refs):
    wp, w1, w2 = refs[:na], refs[na : na + nb], refs[na + nb : na + nb + nc]
    refs = refs[na + nb + nc :]
    send_ref, keep_ref, gp_ref, gb1_ref, gv_ref, dmid_ref, dctx_ref = refs[:7]
    wph, wpl, w1h, w1l, w2h, w2l, g1_ref = refs[7:]

    @pl.when(pl.program_id(0) == 0)
    def _():
        k = load_weight(offs, 0, wp, wph, wpl)
        k = load_weight(offs, k, w1, w1h, w1l)
        load_weight(offs, k, w2, w2h, w2l)
        g1_ref[...] = jnp.zeros_like(g1_ref)
        gp_ref[...] = jnp.zeros_like(gp_ref)
        gb1_ref[...] = jnp.zeros_like(gb1_ref)
        gv_ref[...] = jnp.zeros_like(gv_ref)

    vec = vec_ref[...]
    n2, inv2 = norm_parts(mid_ref[0])
    h2 = n2 * vec[5:6] + vec[6:7]
    dy = dy_ref[0]
    pre = pre_ref[0]
    slope = 0.5 * (1.0 + lax.erf(pre * (1.0 / math.sqrt(2.0)))) + pre * jnp.exp(
        -0.5 * pre * pre
    ) * (1.0 / math.sqrt(2.0 * math.pi))
    dpre = dot3(split(dy), both(w2h, w2l), 1, 1) * slope
    gb1_ref[...] += row_sum(dpre)
    dpre = split(dpre)
    g1_ref[...] += dot3(split(h2), dpre, 0, 0)
    dh2 = dot3(dpre, both(w1h, w1l), 1, 1)
    dmid = dy + norm_back(dh2, n2, inv2, vec[5:6])
    dmid_ref[0] = dmid
    gv_ref[0:1] += row_sum(dmid)
    gv_ref[1:2] += row_sum(dh2 * n2)
    gv_ref[2:3] += row_sum(dh2)
    dmid = split(dmid)
    gp_ref[...] += dot3(split(ctx_ref[0]), dmid, 0, 0)
    dctx_ref[0] = dot3(dmid, both(wph, wpl), 1, 1)

    @pl.when(pl.program_id(0) == pl.num_programs(0) - 1)
    def _():
        part_cols(g1_ref, send_ref, keep_ref, offs[na + nb + nc])


def attn_bwd_kernel(
    np_, offs, x_ref, qkv_ref, ph_ref, pl_ref, ctx_ref, dctx_ref, dmid_ref, vec_ref, *refs
):
    w_pieces = refs[:np_]
    gp_ref, gva_ref, gb1_ref, gb2_ref = refs[np_ : np_ + 4]
    send_ref, keep_ref, gs_ref, dx_ref, wh, wl, dj_ref, g_ref, gv_ref = refs[np_ + 4 :]

    @pl.when(pl.program_id(0) == 0)
    def _():
        load_weight(offs, 0, w_pieces, wh, wl)
        g_ref[...] = jnp.zeros_like(g_ref)
        gv_ref[...] = jnp.zeros_like(gv_ref)

    d = x_ref.shape[2]
    vec = vec_ref[...]
    scale = 1.0 / math.sqrt(HEAD_DIM)
    low = lane_lt((x_ref.shape[1], LANES))
    for j in range(d // LANES):
        sl = slice(j * LANES, (j + 1) * LANES)
        q = qkv_ref[0, :, j * LANES : (j + 1) * LANES] * scale
        k = qkv_ref[0, :, d + j * LANES : d + (j + 1) * LANES]
        v = qkv_ref[0, :, 2 * d + j * LANES : 2 * d + (j + 1) * LANES]
        dc = dctx_ref[0, :, sl]
        prod = dc * ctx_ref[0, :, sl]
        total = jnp.sum(prod, axis=-1, keepdims=True)
        delta0 = jnp.sum(jnp.where(low, prod, 0.0), axis=-1, keepdims=True)
        deltas = (delta0, total - delta0)
        dcs = pair_left(dc, low)
        vs = pair_right(v, low)
        qw, kw, dcw = wide(q), wide(k), wide(dc)
        dq, dk, dv = [], [], []
        for i in range(2):
            ph = ph_ref[0, 2 * j + i]
            p_lo = pl_ref[0, 2 * j + i]
            dp = dot(dcs[i], vs[i], 1, 1)
            ds = (ph.astype(F32) + p_lo.astype(F32)) * (dp - deltas[i])
            dsh, dsl = split(ds)
            dv.append(dot_wide(ph, p_lo, dcw, 0))
            dq.append(dot_wide(dsh, dsl, kw, 1))
            dk.append(dot_wide(dsh, dsl, qw, 0))
        dj_ref[:, sl] = jnp.where(low, dq[0], dq[1]) * scale
        dj_ref[:, d + j * LANES : d + (j + 1) * LANES] = jnp.where(low, dk[0], dk[1])
        dj_ref[:, 2 * d + j * LANES : 2 * d + (j + 1) * LANES] = jnp.where(low, dv[0], dv[1])
    n1, inv1 = norm_parts(x_ref[0])
    h1 = n1 * vec[0:1] + vec[1:2]
    dj = dj_ref[...]
    sums = row_sum(dj)
    gv_ref[2:3] += sums[:, :d]
    gv_ref[3:4] += sums[:, 2 * d :]
    dj = split(dj)
    g_ref[:, : 3 * d] += dot3(split(h1), dj, 0, 0)
    dh1 = dot3(dj, both(wh, wl), 1, 1)
    gv_ref[0:1] += row_sum(dh1 * n1)
    gv_ref[1:2] += row_sum(dh1)
    dx_ref[0] = dmid_ref[0] + norm_back(dh1, n1, inv1, vec[0:1])

    @pl.when(pl.program_id(0) == pl.num_programs(0) - 1)
    def _():
        g_ref[:, 3 * d :] = gp_ref[...]
        part_cols(g_ref, send_ref, keep_ref, offs[np_])
        shards, _, w = gs_ref.shape
        per = gb1_ref.shape[1] // (shards * w)
        for h in range(shards):
            sl = slice(h * w, (h + 1) * w)
            gs_ref[h, 0:4] = gv_ref[0:4, sl]
            gs_ref[h, 4:7] = gva_ref[0:3, sl]
            gs_ref[h, 7:8] = gb2_ref[:, sl]
            for j in range(per):
                at = (h * per + j) * w
                gs_ref[h, 8 + j : 9 + j] = gb1_ref[:, at : at + w]


def per_image(shape):
    n = len(shape)
    return pl.BlockSpec((1,) + tuple(shape[1:]), lambda i, offs: (i,) + (0,) * (n - 1))


def fixed(shape):
    n = len(shape)
    return pl.BlockSpec(tuple(shape), lambda i, offs: (0,) * n)


def run(kernel, name, offs, images, consts, outs, scratch, flops):
    count = images[0].shape[0]
    in_specs = [per_image(a.shape) for a in images] + [fixed(a.shape) for a in consts]
    out_specs = [per_image(s) if im else fixed(s) for s, _, im in outs]
    return pl.pallas_call(
        kernel,
        name=name,
        out_shape=[jax.ShapeDtypeStruct(s, t) for s, t, _ in outs],
        grid_spec=pltpu.PrefetchScalarGridSpec(
            num_scalar_prefetch=1,
            grid=(count,),
            in_specs=in_specs,
            out_specs=out_specs,
            scratch_shapes=scratch,
        ),
        cost_estimate=pl.CostEstimate(flops=flops, transcendentals=0, bytes_accessed=8 << 20),
        compiler_params=pltpu.CompilerParams(
            dimension_semantics=("arbitrary",), vmem_limit_bytes=VMEM_LIMIT
        ),
    )(offs, *images, *consts)


def pair_scratch(rows, cols):
    return [pltpu.VMEM((rows, cols), BF16), pltpu.VMEM((rows, cols), BF16)]


def attn_fwd(x, vec, w):
    offs, pieces = w
    b, s, d = x.shape
    heads = d // HEAD_DIM
    return run(
        lambda *r: attn_fwd_kernel(len(pieces), *r),
        "attn_fwd",
        offs,
        [x],
        [vec, *pieces],
        [
            ((b, s, 3 * d), F32, True),
            ((b, s, d), F32, True),
            ((b, heads, s, s), BF16, True),
            ((b, heads, s, s), BF16, True),
        ],
        pair_scratch(d, 3 * d),
        6 * b * s * d * 3 * d,
    )


def mlp_fwd(x, ctx, dy, vec, b1, ws, core, shards):
    offs = jnp.concatenate([w[0] for w in ws] + [core])
    lists = [w[1] for w in ws]
    n = [len(p) for p in lists]
    b, s, d = x.shape
    ff = b1.shape[1]
    half = ((shards, ff // (2 * shards), d), F32, False)
    return run(
        lambda *r: mlp_fwd_kernel(*n, *r),
        "mlp_fwd",
        offs,
        [x, ctx, dy],
        [vec, b1, *lists[0], *lists[1], *lists[2]],
        [
            ((b, s, d), F32, True),
            ((b, s, ff), F32, True),
            ((b, s, d), F32, True),
            half,
            half,
            ((1, d), F32, False),
        ],
        pair_scratch(d, d)
        + pair_scratch(d, ff)
        + pair_scratch(ff, d)
        + [pltpu.VMEM((ff, d), F32)],
        18 * b * s * d * ff,
    )


def mlp_bwd(ctx, dy, pre, mid, vec, ws, core, shards):
    offs = jnp.concatenate([w[0] for w in ws] + [core])
    lists = [w[1] for w in ws]
    n = [len(p) for p in lists]
    b, s, d = ctx.shape
    ff = pre.shape[2]
    half = ((shards, d // shards, ff // 2), F32, False)
    return run(
        lambda *r: mlp_bwd_kernel(*n, *r),
        "mlp_bwd",
        offs,
        [ctx, dy, pre, mid],
        [vec, *lists[0], *lists[1], *lists[2]],
        [
            half,
            half,
            ((d, d), F32, False),
            ((1, ff), F32, False),
            ((8, d), F32, False),
            ((b, s, d), F32, True),
            ((b, s, d), F32, True),
        ],
        pair_scratch(d, d)
        + pair_scratch(d, ff)
        + pair_scratch(ff, d)
        + [pltpu.VMEM((d, ff), F32)],
        18 * b * s * d * ff,
    )


def attn_bwd(x, qkv, ph, p_lo, ctx, dctx, dmid, vec, w, gwp, gva, gb1, gb2, core, shards):
    offs, pieces = w
    b, s, d = x.shape
    half = ((shards, d // shards, 2 * d), F32, False)
    rows = 8 + gb1.shape[1] // d
    return run(
        lambda *r: attn_bwd_kernel(len(pieces), *r),
        "attn_bwd",
        jnp.concatenate([offs, core]),
        [x, qkv, ph, p_lo, ctx, dctx, dmid],
        [vec, *pieces, gwp, gva, gb1, gb2],
        [half, half, ((shards, rows, d // shards), F32, False), ((b, s, d), F32, True)],
        pair_scratch(d, 3 * d)
        + [pltpu.VMEM((s, 3 * d), F32), pltpu.VMEM((d, 4 * d), F32), pltpu.VMEM((8, d), F32)],
        12 * b * s * d * 3 * d,
    )


def ints(*values):
    return jnp.stack([jnp.asarray(v, jnp.int32) for v in values])


def swap_with(v, n_dp, n_fsdp, dp_bits, fsdp_bits):
    perm = []
    for i in range(n_dp * n_fsdp):
        d, f = divmod(i, n_fsdp)
        perm.append((i, (d ^ dp_bits) * n_fsdp + (f ^ fsdp_bits)))
    return lax.ppermute(v, ("dp", "fsdp"), perm)


class Pairs:
    def __init__(self, n_dp):
        self.n_dp, self.nz = n_dp, n_dp // 4
        dp = lax.axis_index("dp")
        self.core, self.x, self.z = dp % 2, (dp // 2) % 2, dp // 4
        self.y = lax.axis_index("fsdp")

    def over_core(self, v):
        return swap_with(v, self.n_dp, 2, 1, 0)

    def over_x(self, v):
        return swap_with(v, self.n_dp, 2, 2, 0)

    def over_y(self, v):
        return swap_with(v, self.n_dp, 2, 0, 1)

    def over_z(self, v, k):
        return swap_with(v, self.n_dp, 2, 4 * k, 0)

    def gather2(self, w):
        rows = w.shape[0]
        h = rows // 2
        mine = self.over_y(lax.dynamic_slice_in_dim(w, self.core * h, h, 0))
        base = (1 - self.y) * rows
        offs = ints(self.y * rows, base + self.core * h, base + (1 - self.core) * h)
        return offs, [w, mine, self.over_core(mine)]

    def gather4(self, w):
        rows = w.shape[0]
        q = rows // 4
        a = self.over_y(lax.dynamic_slice_in_dim(w, (2 * self.core + self.x) * q, q, 0))
        b = self.over_x(a)
        base = (1 - self.y) * rows
        at = [base + (2 * c + x) * q for c in (self.core, 1 - self.core) for x in (self.x, 1 - self.x)]
        offs = ints(self.y * rows, *at)
        return offs, [w, a, b, self.over_core(a), self.over_core(b)]

    def reduce_small(self, v):
        v = v + self.over_core(v)
        v = pick(v, self.y) + self.over_y(pick(v, 1 - self.y))
        v = v + self.over_x(v)
        parts = [self.over_z(v, k) for k in range(1, self.nz)]
        return v + sum(parts)

    def reduce(self, send, keep):
        n, rows, cols = keep.shape
        got = self.over_core(send)
        sy = pick(got, 1 - self.y) + pick(keep, 1 - self.y)
        ky = pick(got, self.y) + pick(keep, self.y)
        got = self.over_y(sy).reshape(2, rows // 2, cols)
        ky = ky.reshape(2, rows // 2, cols)
        sx = pick(got, 1 - self.x) + pick(ky, 1 - self.x)
        kx = pick(got, self.x) + pick(ky, self.x)
        r = rows // (2 * self.nz)
        got = self.over_x(sx).reshape(self.nz, r, cols)
        kx = kx.reshape(self.nz, r, cols)
        own = pick(got, self.z) + pick(kx, self.z)
        for k in range(1, self.nz):
            to = self.z ^ k
            own = own + self.over_z(pick(got, to) + pick(kx, to), k)
        stack = jnp.stack([own] + [self.over_z(own, k) for k in range(1, self.nz)])
        other = self.over_x(stack)
        return [stack, other, self.over_core(stack), self.over_core(other)]

    def join(self, stacks, name, by_cols):
        nz, r, cols = stacks[0].shape
        rows = 2 * nz * r
        shape = (rows, 2 * cols) if by_cols else (2 * rows, cols)

        def kernel(pos, a, b, c, d, out):
            core, x, z = pos[0], pos[1], pos[2]
            for i, ref in enumerate((a, b, c, d)):
                cc = core if i < 2 else 1 - core
                xx = x if i % 2 == 0 else 1 - x
                for k in range(nz):
                    row = (xx * nz + (z ^ k)) * r
                    if by_cols:
                        col = pl.multiple_of(cc * cols, LANES)
                        out[pl.ds(pl.multiple_of(row, 8), r), pl.ds(col, cols)] = ref[k]
                    else:
                        out[pl.ds(pl.multiple_of(cc * rows + row, 8), r), :] = ref[k]

        return pl.pallas_call(
            kernel,
            name=name,
            out_shape=jax.ShapeDtypeStruct(shape, F32),
            grid_spec=pltpu.PrefetchScalarGridSpec(
                num_scalar_prefetch=1,
                grid=(1,),
                in_specs=[fixed(a.shape) for a in stacks],
                out_specs=fixed(shape),
            ),
        )(ints(self.core, self.x, self.z), *stacks)


def pick(v, i):
    return lax.dynamic_index_in_dim(v, i, 0, keepdims=False)


class Groups:
    def __init__(self, n_fsdp):
        self.shards = n_fsdp
        self.core = 0

    def gather(self, w):
        return ints(0), [lax.all_gather(w, "fsdp", axis=0, tiled=True)]

    gather2 = gather4 = gather

    def total(self, v):
        part = lax.psum_scatter(v, "fsdp", scatter_dimension=0, tiled=True)
        return lax.psum(part, "dp")[0]

    reduce_small = total

    def reduce(self, send, keep):
        return self.total(keep), self.total(send)

    def join(self, parts, name, by_cols):
        return jnp.concatenate(parts, axis=1 if by_cols else 0)


def body(n_dp, n_fsdp, x, g1, s1, wqkv, qb, vb, wproj, pb, g2, s2, wfc1, b1, wfc2, b2, dy):
    pairs = n_fsdp == 2 and n_dp % 4 == 0 and (n_dp & (n_dp - 1)) == 0
    comm = Pairs(n_dp) if pairs and wqkv.shape[0] % (4 * n_dp) == 0 else Groups(n_fsdp)
    w = g1.shape[0]
    small = jnp.concatenate([jnp.stack([g1, s1, qb, vb, pb, g2, s2, b2]), b1.reshape(-1, w)])
    if n_fsdp == 2 and isinstance(comm, Pairs):
        other = comm.over_y(small)
        first = comm.y == 0
        small = jnp.stack([jnp.where(first, small, other), jnp.where(first, other, small)])
    else:
        small = lax.all_gather(small, "fsdp", axis=0)
    vec = small[:, :8].transpose(1, 0, 2).reshape(8, -1)
    b1f = small[:, 8:].reshape(1, -1)
    w_qkv = comm.gather2(wqkv)
    ws = tuple(comm.gather4(v) for v in (wproj, wfc1, wfc2))
    core = ints(comm.core)
    qkv, ctx, ph, p_lo = attn_fwd(x, vec, w_qkv)
    out, pre, mid, send2, keep2, gb2 = mlp_fwd(x, ctx, dy, vec, b1f, ws, core, n_fsdp)
    red2 = comm.reduce(send2, keep2)
    send1, keep1, gwp, gb1, gva, dmid, dctx = mlp_bwd(ctx, dy, pre, mid, vec, ws, core, n_fsdp)
    red1 = comm.reduce(send1, keep1)
    send0, keep0, gs, dx = attn_bwd(
        x, qkv, ph, p_lo, ctx, dctx, dmid, vec, w_qkv, gwp, gva, gb1, gb2, core, n_fsdp
    )
    red0 = comm.reduce(send0, keep0)
    gs = comm.reduce_small(gs)
    gw2 = comm.join(red2, "join_fc2", False)
    gw1 = comm.join(red1, "join_fc1", True)
    ga = comm.join(red0, "join_attn", True)
    d = x.shape[2]
    return (
        out,
        dx,
        gs[0],
        gs[1],
        ga[:, : 3 * d],
        gs[2],
        gs[3],
        ga[:, 3 * d :],
        gs[4],
        gs[5],
        gs[6],
        gw1,
        gs[8:].reshape(-1),
        gw2,
        gs[7],
    )


def solution(mesh):
    n_dp, n_fsdp = mesh.shape["dp"], mesh.shape["fsdp"]
    act = P(("dp", "fsdp"), None, None)
    vec = P("fsdp")
    mat = P("fsdp", None)
    in_specs = (act, vec, vec, mat, vec, vec, mat, vec, vec, vec, mat, vec, mat, vec, act)
    out_specs = (act,) + in_specs[:1] + in_specs[1:14]
    return jax.shard_map(
        lambda *a: body(n_dp, n_fsdp, *a),
        mesh=mesh,
        in_specs=in_specs,
        out_specs=out_specs,
        check_vma=False,
    )
```

```python
import math

import jax
import jax.numpy as jnp
from jax import lax
from jax.experimental import pallas as pl
from jax.experimental.pallas import tpu as pltpu
from jax.sharding import PartitionSpec as P


HEAD_DIM = 64
LANES = 128
EPS = 1e-06
F32 = jnp.float32
BF16 = jnp.bfloat16
VMEM_LIMIT = 56 * 1024 * 1024


def split(v):
    hi = v.astype(BF16)
    lo = (v - hi.astype(F32)).astype(BF16)
    return hi, lo


def dot(a, b, ca, cb):
    return lax.dot_general(a, b, (((ca,), (cb,)), ((), ())), preferred_element_type=F32)


def dot3(a, b, ca, cb):
    ah, al = a
    bh, bl = b
    return dot(ah, bh, ca, cb) + (dot(ah, bl, ca, cb) + dot(al, bh, ca, cb))


def row_sum(v):
    return jnp.sum(v, axis=0, keepdims=True)


def norm_parts(v):
    center = v - jnp.mean(v, axis=-1, keepdims=True)
    inv = lax.rsqrt(jnp.mean(center * center, axis=-1, keepdims=True) + EPS)
    return center * inv, inv


def norm_back(dh, n, inv, gain):
    s = dh * gain
    return inv * (
        s - jnp.mean(s, axis=-1, keepdims=True) - n * jnp.mean(s * n, axis=-1, keepdims=True)
    )


def load_weight(offs, k, pieces, hi_ref, lo_ref):
    for p in pieces:
        at = pl.multiple_of(offs[k], 16)
        hi, lo = split(p[...])
        hi_ref[pl.ds(at, p.shape[0]), :] = hi
        lo_ref[pl.ds(at, p.shape[0]), :] = lo
        k += 1
    return k


def load_rows(offs, k, pieces, ref):
    n = ref.shape[0] // 3
    for p in pieces:
        hi, lo = split(p[...])
        for base, part in ((0, hi), (n, hi), (2 * n, lo)):
            ref[pl.ds(pl.multiple_of(base + offs[k], 16), p.shape[0]), :] = part
        k += 1


def load_cols(offs, k, pieces, ref):
    n = ref.shape[1] // 3
    for p in pieces:
        at = pl.ds(pl.multiple_of(offs[k], 16), p.shape[0])
        hi, lo = split(p[...])
        ref[at, :n] = hi
        ref[at, n : 2 * n] = hi
        ref[at, 2 * n :] = lo
        k += 1


def tall(v):
    hi, lo = split(v)
    return jnp.concatenate([hi, lo, hi], axis=1)


def fold(t):
    n = t.shape[1] // 2
    return t[:, :n] + t[:, n:]


def dot_rows(v, w3):
    hi, lo = split(v)
    n = w3.shape[0] // 3
    return fold(dot(hi, w3[n:], 1, 1)) + dot(lo, w3[:n], 1, 1)


def dot_outer(v3, w):
    n = v3.shape[1] // 3
    t = dot(v3[:, : 2 * n], w[0], 0, 0)
    return t[:n] + (t[n:] + dot(v3[:, :n], w[1], 0, 0))


def both(hi_ref, lo_ref):
    return hi_ref[...], lo_ref[...]


def lane_lt(shape):
    return lax.broadcasted_iota(jnp.int32, shape, 1) < HEAD_DIM


def swap(v):
    return pltpu.roll(v, HEAD_DIM, 1)


def pair_left(v, low):
    hi = v.astype(BF16).astype(F32)
    lo = v - hi
    zero = jnp.zeros_like(v)
    h0 = jnp.concatenate([jnp.where(low, hi, swap(lo)), jnp.where(low, hi, zero)], axis=1)
    h1 = jnp.concatenate([jnp.where(low, swap(lo), hi), jnp.where(low, zero, hi)], axis=1)
    return h0.astype(BF16), h1.astype(BF16)


def pair_right(v, low):
    hi = v.astype(BF16).astype(F32)
    lo = v - hi
    rolled = swap(hi)
    h0 = jnp.concatenate([jnp.where(low, hi, rolled), lo], axis=1)
    h1 = jnp.concatenate([jnp.where(low, rolled, hi), lo], axis=1)
    return h0.astype(BF16), h1.astype(BF16)


def wide(v):
    hi, lo = split(v)
    return hi, jnp.concatenate([hi, lo], axis=1)


def dot_wide(ph, pl_, w, ca):
    hi, cat = w
    t = dot(ph, cat, ca, 0)
    return t[:, :LANES] + (t[:, LANES:] + dot(pl_, hi, ca, 0))


def part_rows(g_ref, send_ref, keep_ref, core):
    n, rows, cols = keep_ref.shape
    for i in range(n):
        lanes = slice(i * cols, (i + 1) * cols)
        send_ref[i] = g_ref[pl.ds(pl.multiple_of((1 - core) * rows, 8), rows), lanes]
        keep_ref[i] = g_ref[pl.ds(pl.multiple_of(core * rows, 8), rows), lanes]


def part_cols(g_ref, send_ref, keep_ref, core):
    n, rows, cols = keep_ref.shape
    for i in range(n):
        at = pl.multiple_of((1 - core) * cols, LANES)
        send_ref[i] = g_ref[i * rows : (i + 1) * rows, pl.ds(at, cols)]
        at = pl.multiple_of(core * cols, LANES)
        keep_ref[i] = g_ref[i * rows : (i + 1) * rows, pl.ds(at, cols)]


def last():
    return pl.program_id(0) == pl.num_programs(0) - 1


def first():
    return pl.program_id(0) == 0


def qkv_kernel(np_, offs, x_ref, vec_ref, *refs):
    w_pieces = refs[:np_]
    qkv_ref, w3 = refs[np_:]

    @pl.when(first())
    def _():
        load_rows(offs, 0, w_pieces, w3)

    d = x_ref.shape[2]
    vec = vec_ref[...]
    n1, _ = norm_parts(x_ref[0])
    h1 = n1 * vec[0:1] + vec[1:2]
    qkv = dot(tall(h1), w3[...], 1, 0)
    qkv_ref[0, :, :d] = qkv[:, :d] + vec[2:3]
    qkv_ref[0, :, d : 2 * d] = qkv[:, d : 2 * d]
    qkv_ref[0, :, 2 * d :] = qkv[:, 2 * d :] + vec[3:4]


def attn_fwd_kernel(offs, qkv_ref, ctx_ref, ph_ref, pl_ref):
    d = ctx_ref.shape[2]
    low = lane_lt((qkv_ref.shape[1], LANES))
    for j in range(d // LANES):
        sl = slice(j * LANES, (j + 1) * LANES)
        q = qkv_ref[0, :, sl] * (1.0 / math.sqrt(HEAD_DIM))
        k = qkv_ref[0, :, d + j * LANES : d + (j + 1) * LANES]
        v = qkv_ref[0, :, 2 * d + j * LANES : 2 * d + (j + 1) * LANES]
        qs = pair_left(q, low)
        ks = pair_right(k, low)
        vw = wide(v)
        outs = []
        for i in range(2):
            s = dot(qs[i], ks[i], 1, 1)
            e = jnp.exp(s - jnp.max(s, axis=-1, keepdims=True))
            p = e * (1.0 / jnp.sum(e, axis=-1, keepdims=True))
            hi, lo = split(p)
            ph_ref[0, 2 * j + i] = hi
            pl_ref[0, 2 * j + i] = lo
            outs.append(dot_wide(hi, lo, vw, 1))
        ctx_ref[0, :, sl] = jnp.where(low, outs[0], outs[1])


def fill_rows(buf_ref, ref):
    n, s, _ = ref.shape
    step = buf_ref.shape[0] // n
    buf_ref[...] = jnp.zeros_like(buf_ref)
    for i in range(n):
        buf_ref[i * step : i * step + s, :] = ref[i]


def take_rows(ref, rows_ref):
    n, s, _ = ref.shape
    step = rows_ref.shape[0] // n
    for i in range(n):
        ref[i] = rows_ref[i * step : i * step + s, :]


def mlp_kernel(np_, offs, x_ref, ctx_ref, dy_ref, vec_ref, b1_ref, wp, w1, *refs):
    n, n2 = np_
    pp, p1, p2 = refs[:n], refs[n : 2 * n], refs[2 * n : 2 * n + n2]
    refs = refs[2 * n + n2 :]
    out_ref, mid_ref, dh2_ref, gb1_ref, gb2_ref = refs[:5]
    send2_ref, keep2_ref, send1_ref, keep1_ref = refs[5:9]
    wph, wpl, w1r, w2c, h3, y3, mids, outs, dh2s, g2_ref, g1_ref = refs[9:]
    i = pl.program_id(0)
    d = x_ref.shape[2]
    cols = b1_ref.shape[1]
    at = pl.ds(pl.multiple_of(i * cols, LANES), cols)

    @pl.when(first())
    def _():
        vec = vec_ref[...]
        load_weight(offs, 0, [wp, *pp], wph, wpl)
        load_cols(offs, n + 1, p2, w2c)
        fill_rows(outs, ctx_ref)
        fill_rows(mids, x_ref)
        mid = mids[...] + dot3(split(outs[...]), both(wph, wpl), 1, 0) + vec[4:5]
        mids[...] = mid
        n2, _ = norm_parts(mid)
        h3[...] = tall(n2 * vec[5:6] + vec[6:7])
        fill_rows(dh2s, dy_ref)
        dy = dh2s[...]
        y3[...] = tall(dy)
        gb2_ref[...] = row_sum(dy)
        outs[...] = mid + vec[7:8]
        dh2s[...] = jnp.zeros_like(dh2s)

    load_rows(offs, 0, [w1, *p1], w1r)
    pre = dot(h3[...], w1r[...], 1, 0) + b1_ref[...]
    half = 0.5 * (1.0 + lax.erf(pre * (1.0 / math.sqrt(2.0))))
    act = split(pre * half)
    slope = half + pre * jnp.exp(-0.5 * pre * pre) * (1.0 / math.sqrt(2.0 * math.pi))
    outs[...] += fold(dot(act[0], w2c[at, d:], 1, 0)) + dot(act[1], w2c[at, :d], 1, 0)
    g2_ref[:, at] = dot_outer(y3[...], act)
    dpre = dot(y3[...], w2c[at, :], 1, 1) * slope
    gb1_ref[...] = row_sum(dpre)
    dh2s[...] += dot_rows(dpre, w1r[...])
    g1_ref[:, at] = dot_outer(h3[...], split(dpre))

    @pl.when(last())
    def _():
        take_rows(out_ref, outs)
        take_rows(mid_ref, mids)
        take_rows(dh2_ref, dh2s)
        core = offs[n + 1 + len(p2)]
        part_rows(g2_ref, send2_ref, keep2_ref, core)
        part_cols(g1_ref, send1_ref, keep1_ref, core)


def mid_kernel(np_, offs, dh2_ref, ctx_ref, dy_ref, mid_ref, vec_ref, *refs):
    gp_ref, gv_ref, dmid_ref, dctx_ref, wph, wpl = refs[np_:]

    @pl.when(first())
    def _():
        load_weight(offs, 0, refs[:np_], wph, wpl)
        gp_ref[...] = jnp.zeros_like(gp_ref)
        gv_ref[...] = jnp.zeros_like(gv_ref)

    n2, inv2 = norm_parts(mid_ref[0])
    dh2 = dh2_ref[0]
    dmid = dy_ref[0] + norm_back(dh2, n2, inv2, vec_ref[5:6])
    dmid_ref[0] = dmid
    gv_ref[0:1] += row_sum(dmid)
    gv_ref[1:2] += row_sum(dh2 * n2)
    gv_ref[2:3] += row_sum(dh2)
    dmid = split(dmid)
    gp_ref[...] += dot3(split(ctx_ref[0]), dmid, 0, 0)
    dctx_ref[0] = dot3(dmid, both(wph, wpl), 1, 1)


def attn_bwd_kernel(
    offs, x_ref, qkv_ref, ph_ref, pl_ref, ctx_ref, dctx_ref, vec_ref, gp_ref, *refs
):
    dj_ref, send_ref, keep_ref, g_ref = refs
    d = ctx_ref.shape[2]

    @pl.when(first())
    def _():
        g_ref[:, : 3 * d] = jnp.zeros((d, 3 * d), F32)
        g_ref[:, 3 * d :] = gp_ref[...]

    scale = 1.0 / math.sqrt(HEAD_DIM)
    low = lane_lt((ctx_ref.shape[1], LANES))
    for j in range(d // LANES):
        sl = slice(j * LANES, (j + 1) * LANES)
        q = qkv_ref[0, :, j * LANES : (j + 1) * LANES] * scale
        k = qkv_ref[0, :, d + j * LANES : d + (j + 1) * LANES]
        v = qkv_ref[0, :, 2 * d + j * LANES : 2 * d + (j + 1) * LANES]
        dc = dctx_ref[0, :, sl]
        prod = dc * ctx_ref[0, :, sl]
        delta0 = jnp.sum(jnp.where(low, prod, 0.0), axis=-1, keepdims=True)
        delta1 = jnp.sum(jnp.where(low, 0.0, prod), axis=-1, keepdims=True)
        deltas = (delta0, delta1)
        dcs = pair_left(dc, low)
        vs = pair_right(v, low)
        qw, kw, dcw = wide(q), wide(k), wide(dc)
        dq, dk, dv = [], [], []
        for i in range(2):
            ph = ph_ref[0, 2 * j + i]
            p_lo = pl_ref[0, 2 * j + i]
            dp = dot(dcs[i], vs[i], 1, 1)
            ds = (ph.astype(F32) + p_lo.astype(F32)) * (dp - deltas[i])
            dsh, dsl = split(ds)
            dv.append(dot_wide(ph, p_lo, dcw, 0))
            dq.append(dot_wide(dsh, dsl, kw, 1))
            dk.append(dot_wide(dsh, dsl, qw, 0))
        dj_ref[0, :, sl] = jnp.where(low, dq[0], dq[1]) * scale
        dj_ref[0, :, d + j * LANES : d + (j + 1) * LANES] = jnp.where(low, dk[0], dk[1])
        dj_ref[0, :, 2 * d + j * LANES : 2 * d + (j + 1) * LANES] = jnp.where(low, dv[0], dv[1])
    n1, _ = norm_parts(x_ref[0])
    h1 = n1 * vec_ref[0:1] + vec_ref[1:2]
    g_ref[:, : 3 * d] += dot_outer(tall(h1), split(dj_ref[0]))

    @pl.when(last())
    def _():
        part_cols(g_ref, send_ref, keep_ref, offs[0])


def input_grad_kernel(np_, offs, x_ref, dj_ref, dmid_ref, vec_ref, *refs):
    w_pieces = refs[:np_]
    gva_ref, gb1_ref, gb2_ref = refs[np_ : np_ + 3]
    gs_ref, dx_ref, w3, gv_ref = refs[np_ + 3 :]

    @pl.when(first())
    def _():
        load_rows(offs, 0, w_pieces, w3)
        gv_ref[...] = jnp.zeros_like(gv_ref)

    d = x_ref.shape[2]
    n1, inv1 = norm_parts(x_ref[0])
    dj = dj_ref[0]
    sums = row_sum(dj)
    gv_ref[2:3] += sums[:, :d]
    gv_ref[3:4] += sums[:, 2 * d :]
    dh1 = dot_rows(dj, w3[...])
    gv_ref[0:1] += row_sum(dh1 * n1)
    gv_ref[1:2] += row_sum(dh1)
    dx_ref[0] = dmid_ref[0] + norm_back(dh1, n1, inv1, vec_ref[0:1])

    @pl.when(last())
    def _():
        shards, _, w = gs_ref.shape
        per = gb1_ref.shape[1] // (shards * w)
        for h in range(shards):
            sl = slice(h * w, (h + 1) * w)
            gs_ref[h, 0:4] = gv_ref[0:4, sl]
            gs_ref[h, 4:7] = gva_ref[0:3, sl]
            gs_ref[h, 7:8] = gb2_ref[:, sl]
            for j in range(per):
                at = (h * per + j) * w
                gs_ref[h, 8 + j : 9 + j] = gb1_ref[:, at : at + w]


def per_image(shape):
    n = len(shape)
    return pl.BlockSpec((1,) + tuple(shape[1:]), lambda i, offs: (i,) + (0,) * (n - 1))


def fixed(shape):
    n = len(shape)
    return pl.BlockSpec(tuple(shape), lambda i, offs: (0,) * n)


def block_at(shape, col):
    return pl.BlockSpec(shape, lambda i, offs: (0, col))


def run(kernel, offs, images, consts, outs, scratch, flops, blocks={}):
    count = images[0].shape[0]
    in_specs = [per_image(a.shape) for a in images] + [
        block_at(*blocks[i]) if i in blocks else fixed(a.shape) for i, a in enumerate(consts)
    ]
    out_specs = [per_image(s) if im else fixed(s) for s, _, im in outs]
    return pl.pallas_call(
        kernel,
        out_shape=[jax.ShapeDtypeStruct(s, t) for s, t, _ in outs],
        grid_spec=pltpu.PrefetchScalarGridSpec(
            num_scalar_prefetch=1,
            grid=(count,),
            in_specs=in_specs,
            out_specs=out_specs,
            scratch_shapes=scratch,
        ),
        cost_estimate=pl.CostEstimate(flops=flops, transcendentals=0, bytes_accessed=8 << 20),
        compiler_params=pltpu.CompilerParams(
            dimension_semantics=("arbitrary",), vmem_limit_bytes=VMEM_LIMIT
        ),
    )(offs, *images, *consts)


def pair_scratch(rows, cols):
    return [pltpu.VMEM((rows, cols), BF16), pltpu.VMEM((rows, cols), BF16)]


def image(*shape, dtype=F32):
    return (shape, dtype, True)


def const(*shape):
    return (shape, F32, False)


def qkv_call(x, vec, w):
    offs, pieces = w
    b, s, d = x.shape
    return run(
        lambda *r: qkv_kernel(len(pieces), *r),
        offs,
        [x],
        [vec, *pieces],
        [image(b, s, 3 * d)],
        [pltpu.VMEM((3 * d, 3 * d), BF16)],
        18 * b * s * d * d,
    )[0]


def attn_fwd(qkv, zero):
    b, s, d = qkv.shape
    d = d // 3
    heads = d // HEAD_DIM
    probs = image(b, heads, s, s, dtype=BF16)
    return run(
        attn_fwd_kernel, zero, [qkv], [], [image(b, s, d), probs, probs], [],
        30 * b * s * d * d,
    )


def cols_block(shape, cols, at):
    return pl.BlockSpec((shape[0], cols), lambda i, offs: (0, at(i)))


def mlp(x, ctx, dy, vec, b1, joint, w2, core, shards):
    offs, (wp, w1, *pieces) = joint
    b, s, d = x.shape
    ff = b1.shape[1]
    rows = b * (-(-s // 8) * 8)
    c = ff // 3
    half2, half1 = (shards, d // 2, ff // shards), (shards, d // shards, ff // 2)
    shapes = [(b, s, d), (b, s, d), (b, s, d), (1, ff), (1, d), half2, half2, half1, half1]
    n = len(pieces)
    specs = [fixed(a.shape) for a in (x, ctx, dy, vec)]
    specs += [cols_block(b1.shape, c, lambda i: i), fixed(wp.shape)]
    specs += [cols_block(w1.shape, c, lambda i: i)]
    specs += [cols_block(p.shape, d, lambda i: ff // d) for p in pieces]
    specs += [cols_block(p.shape, c, lambda i: i) for p in pieces]
    specs += [fixed(p.shape) for p in w2[1]]
    out_specs = [fixed(t) for t in shapes]
    out_specs[3] = cols_block((1, ff), c, lambda i: i)
    big = pltpu.VMEM((rows, d), F32)
    tall_one = pltpu.VMEM((rows, 3 * d), BF16)
    return pl.pallas_call(
        lambda *r: mlp_kernel((n, len(w2[1])), *r),
        name="mlp",
        out_shape=[jax.ShapeDtypeStruct(t, F32) for t in shapes],
        grid_spec=pltpu.PrefetchScalarGridSpec(
            num_scalar_prefetch=1,
            grid=(ff // c,),
            in_specs=specs,
            out_specs=out_specs,
            scratch_shapes=pair_scratch(d, d)
            + [pltpu.VMEM((3 * d, c), BF16), pltpu.VMEM((ff, 3 * d), BF16)]
            + [tall_one, tall_one, big, big, big]
            + [pltpu.VMEM((d, ff), F32)] * 2,
        ),
        cost_estimate=pl.CostEstimate(
            flops=40 * b * s * d * ff, transcendentals=0, bytes_accessed=8 << 20
        ),
        compiler_params=pltpu.CompilerParams(
            dimension_semantics=("arbitrary",), vmem_limit_bytes=VMEM_LIMIT
        ),
    )(
        jnp.concatenate([offs, w2[0], core]),
        *(x, ctx, dy, vec, b1, wp, w1),
        *pieces,
        *pieces,
        *w2[1],
    )


def mlp_mid(dh2, ctx, dy, mid, vec, joint):
    offs, (wp, _, *pieces) = joint
    b, s, d = mid.shape
    return run(
        lambda *r: mid_kernel(1 + len(pieces), *r),
        offs,
        [dh2, ctx, dy, mid],
        [vec, wp, *pieces],
        [const(d, d), const(8, d), image(b, s, d), image(b, s, d)],
        pair_scratch(d, d),
        12 * b * s * d * d,
        {2 + i: ((p.shape[0], d), p.shape[1] // d - 1) for i, p in enumerate(pieces)},
    )


def attn_bwd(x, qkv, ph, p_lo, ctx, dctx, vec, gwp, core, shards):
    b, s, d = ctx.shape
    half = const(shards, d // shards, 2 * d)
    return run(
        attn_bwd_kernel,
        core,
        [x, qkv, ph, p_lo, ctx, dctx],
        [vec, gwp],
        [image(b, s, 3 * d), half, half],
        [pltpu.VMEM((d, 4 * d), F32)],
        60 * b * s * d * d,
    )


def input_grad(x, dj, dmid, vec, w, gva, gb1, gb2, shards):
    offs, pieces = w
    b, s, d = x.shape
    rows = 8 + gb1.shape[1] // d
    return run(
        lambda *r: input_grad_kernel(len(pieces), *r),
        offs,
        [x, dj, dmid],
        [vec, *pieces, gva, gb1, gb2],
        [const(shards, rows, d // shards), image(b, s, d)],
        [pltpu.VMEM((3 * d, 3 * d), BF16), pltpu.VMEM((8, d), F32)],
        18 * b * s * d * d,
    )


def tie(v, *after):
    return lax.optimization_barrier((v, *after))[0]


def ints(*values):
    return jnp.stack([jnp.asarray(v, jnp.int32) for v in values])


def swap_with(v, n_dp, n_fsdp, dp_bits, fsdp_bits):
    perm = []
    for i in range(n_dp * n_fsdp):
        d, f = divmod(i, n_fsdp)
        perm.append((i, (d ^ dp_bits) * n_fsdp + (f ^ fsdp_bits)))
    return lax.ppermute(v, ("dp", "fsdp"), perm)


class Pairs:
    def __init__(self, n_dp):
        self.n_dp, self.nz = n_dp, n_dp // 4
        self.bits = self.nz.bit_length() - 1
        dp = lax.axis_index("dp")
        self.core, self.x, self.z = dp % 2, (dp // 2) % 2, dp // 4
        self.y = lax.axis_index("fsdp")

    def over_core(self, v):
        return swap_with(v, self.n_dp, 2, 1, 0)

    def over_x(self, v):
        return swap_with(v, self.n_dp, 2, 2, 0)

    def over_y(self, v):
        return swap_with(v, self.n_dp, 2, 0, 1)

    def over_z(self, v, k):
        return swap_with(v, self.n_dp, 2, 4 * k, 0)

    def quarter(self, w):
        rows = w.shape[0] // 4
        return lax.dynamic_slice_in_dim(w, (2 * self.core + self.x) * rows, rows, 0)

    def quarter_offs(self, rows):
        base = (1 - self.y) * rows
        q = rows // 4
        order = [(c, x) for c in (self.core, 1 - self.core) for x in (self.x, 1 - self.x)]
        return ints(self.y * rows, *(base + (2 * c + x) * q for c, x in order))

    def finish(self, a):
        b = self.over_x(a)
        return [a, b, self.over_core(a), self.over_core(b)]

    def halve(self, axis, at, got, keep):
        both = [pick(got, i, axis) + pick(keep, i, axis) for i in (1 - at, at)]
        return both[0], both[1]

    def halve_x(self, got, keep):
        shape = keep.shape
        shape = shape[:-2] + (2, shape[-2] // 2, shape[-1])
        return self.halve(len(shape) - 3, self.x, got.reshape(shape), keep.reshape(shape))

    def halve_z(self, bit, got, keep):
        shape = keep.shape
        shape = shape[:-3] + (shape[-3] // 2, 2) + shape[-2:]
        at = (self.z // (1 << bit)) % 2
        return self.halve(len(shape) - 3, at, got.reshape(shape), keep.reshape(shape))

    def reduce_z(self, got, keep, small=None):
        shape = keep.shape
        shape = shape[:-2] + (self.nz, shape[-2] // self.nz, shape[-1])
        got, keep = got.reshape(shape), keep.reshape(shape)
        for bit in range(self.bits):
            send, keep = self.halve_z(bit, got, keep)
            if small is not None:
                send, small = lax.optimization_barrier((send, small))
                small = small + self.over_z(small, 1 << bit)
            got = self.over_z(send, 1 << bit)
        total = got + keep
        total = total.reshape(total.shape[:-3] + total.shape[-2:])
        return total if small is None else (total, small)

    def gather_z(self, v, bits):
        for bit in bits:
            v = jnp.stack([v, self.over_z(v, 1 << bit)])
        return v

    def placed(self, bits, with_x):
        out = []
        names = list(bits) + (["x"] if with_x else [])
        for i in range(1 << len(names)):
            at = [(i >> k) & 1 for k in range(len(names))]
            dz = sum(a << n for a, n in zip(at, names) if n != "x")
            dx = sum(a for a, n in zip(at, names) if n == "x")
            out.append((dx, dz))
        return out

    def join(self, stacks, moves, put, outs, scratch=(), finish=None):
        nz = self.nz
        n_out = len(outs)

        def kernel(pos, *refs):
            ins, refs = refs[: len(stacks)], refs[len(stacks) :]
            for core in range(2):

                @pl.when(pos[0] == core)
                def _():
                    for ref, places in zip(ins, moves):
                        for k, (dc, dx, dz) in enumerate(places):
                            row = (pos[1] ^ dx) * nz + (pos[2] ^ dz)
                            put(ref.at[k], core ^ dc, row, refs)

            if finish is not None:
                finish(refs)

        return pl.pallas_call(
            kernel,
            out_shape=[jax.ShapeDtypeStruct(s, F32) for s in outs],
            grid_spec=pltpu.PrefetchScalarGridSpec(
                num_scalar_prefetch=1,
                grid=(1,),
                in_specs=[fixed(a.shape) for a in stacks],
                out_specs=[fixed(s) for s in outs],
                scratch_shapes=list(scratch),
            ),
            compiler_params=pltpu.CompilerParams(vmem_limit_bytes=VMEM_LIMIT),
        )(ints(self.core, self.x, self.z), *stacks)

    def join_attn(self, stacks, moves, d):
        _, r, cols = stacks[0].shape
        rows = 2 * self.nz * r

        def put(ref, core, row, refs):
            at = pl.ds(pl.multiple_of(row * r, 8), r)
            if core == 0:
                refs[0][at, :cols] = ref[...]
            else:
                n = 3 * d - cols
                refs[0][at, cols:] = ref[:, :n]
                refs[1][at, :] = ref[:, n:]

        return self.join(stacks, moves, put, [(rows, 3 * d), (rows, d)])

    def join_mlp(self, stacks, moves):
        _, _, r, cols = stacks[0].shape
        rows = 2 * self.nz * r

        def put(ref, core, row, refs):
            at = pl.multiple_of(row * r, 8)
            refs[2][pl.ds(core * rows + at, r), :] = ref[0]
            refs[1][pl.ds(at, r), core * cols : (core + 1) * cols] = ref[1]

        def finish(refs):
            refs[0][...] = refs[2][...].T

        outs = [(cols, 2 * rows), (rows, 2 * cols)]
        scratch = [pltpu.VMEM((2 * rows, cols), F32)]
        return self.join(stacks, moves, put, outs, scratch, finish)


def pick(v, i, axis=0):
    return lax.dynamic_index_in_dim(v, i, axis, keepdims=False)


def whole_mesh_step(n_fsdp, x, vec, b1f, wqkv, wproj, wfc1, wfc2, dy):
    def gather(w):
        return lax.all_gather(w, "fsdp", axis=0, tiled=True)

    def total(v):
        part = lax.psum_scatter(v, "fsdp", scatter_dimension=0, tiled=True)
        return lax.psum(part, "dp")[0]

    zero = ints(0)
    d = x.shape[2]
    w_qkv, w_2 = (zero, [gather(wqkv)]), (zero, [gather(wfc2)])
    joint = zero, [gather(wproj), gather(wfc1)]
    qkv = qkv_call(x, vec, w_qkv)
    ctx, ph, p_lo = attn_fwd(qkv, zero)
    out, mid, dh2, gb1, gb2, send2, keep2, send1, keep1 = mlp(
        x, ctx, dy, vec, b1f, joint, w_2, zero, n_fsdp
    )
    gwp, gva, dmid, dctx = mlp_mid(dh2, ctx, dy, mid, vec, joint)
    dj, send0, keep0 = attn_bwd(x, qkv, ph, p_lo, ctx, dctx, vec, gwp, zero, n_fsdp)
    gs, dx = input_grad(x, dj, dmid, vec, w_qkv, gva, gb1, gb2, n_fsdp)
    ga = jnp.concatenate([total(keep0), total(send0)], axis=1)
    gw1 = jnp.concatenate([total(keep1), total(send1)], axis=1)
    gw2 = jnp.concatenate([total(keep2), total(send2)], axis=0).T
    return out, dx, ga[:, : 3 * d], ga[:, 3 * d :], gw1, gw2, total(gs)


def pair_step(n_dp, x, vec, b1f, wqkv, wproj, wfc1, wfc2, dy):
    c = Pairs(n_dp)
    core = ints(c.core)
    d = x.shape[2]
    came = c.over_y(c.quarter(wqkv))
    w_qkv = c.quarter_offs(wqkv.shape[0]), [wqkv, *c.finish(came)]
    joint = tie(jnp.concatenate([c.quarter(wfc1), c.quarter(wproj)], axis=1), came)
    joint = c.over_y(joint)
    w_2 = c.over_y(tie(c.quarter(wfc2), came))
    qkv = qkv_call(x, vec, w_qkv)
    pieces = c.finish(tie(joint, qkv))
    joint = c.quarter_offs(wproj.shape[0]), [wproj, wfc1, *pieces]
    ctx, ph, p_lo = attn_fwd(qkv, core)
    w_2 = c.quarter_offs(wfc2.shape[0]), [wfc2, *c.finish(tie(w_2, qkv))]
    out, mid, dh2, gb1, gb2, send2, keep2, send1, keep1 = mlp(
        x, ctx, dy, vec, b1f, joint, w_2, core, 2
    )
    got2 = c.over_core(send2)
    got1 = c.over_core(send1)
    gwp, gva, dmid, dctx = mlp_mid(dh2, ctx, dy, mid, vec, joint)
    send2, keep2 = c.halve_x(got2, keep2)
    send1, keep1 = c.halve(0, c.y, got1, keep1)
    got2 = c.over_x(send2)
    got1 = c.over_y(send1)
    dctx = tie(dctx, send1, keep1, send2, keep2)
    dj, send0, keep0 = attn_bwd(x, qkv, ph, p_lo, ctx, dctx, vec, gwp, core, 2)
    got0 = c.over_core(send0)
    send2, keep2 = c.halve(0, c.y, got2, keep2)
    send1, keep1 = c.halve_x(got1, keep1)
    got2 = c.over_y(send2)
    got1 = c.over_x(send1)
    dj = tie(dj, send0, send1, keep1, send2, keep2)
    gs, dx = input_grad(x, dj, dmid, vec, w_qkv, gva, gb1, gb2, 2)
    send0, keep0 = c.halve(0, c.y, got0, keep0)
    got0 = c.over_y(send0)
    gs = tie(gs, send0)
    gs = gs + c.over_core(gs)
    gs_got = c.over_y(pick(gs, 1 - c.y))
    gs = pick(gs, c.y)
    gotf, keepf = jnp.stack([got2, got1]), jnp.stack([keep2, keep1])
    f = c.reduce_z(gotf, keepf)
    up = tuple(range(c.bits))
    f = c.gather_z(f, up[::-1])
    gs = gs + gs_got
    gs_got = c.over_x(gs)
    send0, keep0 = c.halve_x(got0, keep0)
    got0 = c.over_x(tie(send0, gs))
    gs = gs + gs_got
    a, gs = c.reduce_z(got0, keep0, gs)
    a = c.gather_z(tie(a, gs), up[:0:-1])
    a = jnp.stack([a, c.over_x(a)])
    a = a.reshape((-1,) + a.shape[-2:])
    fr = f.reshape((-1,) + f.shape[-3:])
    f = [fr, c.over_x(fr)]
    f = f + [c.over_core(v) for v in f]
    pf = c.placed(up[::-1], False)
    pa = c.placed(up[:0:-1], True)
    mf = [[(i // 2, i % 2, dz) for _, dz in pf] for i in range(4)]
    ma = [[(i // 2, dx_, dz ^ (i % 2)) for dx_, dz in pa] for i in range(4)]
    gw2, gw1 = c.join_mlp(f, mf)
    a = [a, c.over_z(a, 1)]
    a = a + [c.over_core(v) for v in a]
    gwqkv, gwproj = c.join_attn(a, ma, d)
    return out, dx, gwqkv, gwproj, gw1, gw2, gs


def is_pairs(n_dp, n_fsdp):
    return n_fsdp == 2 and n_dp >= 8 and (n_dp & (n_dp - 1)) == 0


def body(n_dp, n_fsdp, x, g1, s1, wqkv, qb, vb, wproj, pb, g2, s2, wfc1, b1, wfc2, b2, dy):
    pairs = is_pairs(n_dp, n_fsdp)
    w = g1.shape[0]
    small = jnp.concatenate([jnp.stack([g1, s1, qb, vb, pb, g2, s2, b2]), b1.reshape(-1, w)])
    if pairs:
        other = swap_with(small, n_dp, n_fsdp, 0, 1)
        is_first = lax.axis_index("fsdp") == 0
        small = jnp.stack([jnp.where(is_first, small, other), jnp.where(is_first, other, small)])
    else:
        small = lax.all_gather(small, "fsdp", axis=0)
    vec = small[:, :8].transpose(1, 0, 2).reshape(8, -1)
    b1f = small[:, 8:].reshape(1, -1)
    args = (x, vec, b1f, wqkv, wproj, wfc1, wfc2, dy)
    step = pair_step(n_dp, *args) if pairs else whole_mesh_step(n_fsdp, *args)
    out, dx, gwqkv, gwproj, gw1, gw2, gs = step
    return (
        out,
        dx,
        gs[0],
        gs[1],
        gwqkv,
        gs[2],
        gs[3],
        gwproj,
        gs[4],
        gs[5],
        gs[6],
        gw1,
        gs[8:].reshape(-1),
        gw2,
        gs[7],
    )


def solution(mesh):
    n_dp, n_fsdp = mesh.shape["dp"], mesh.shape["fsdp"]
    act = P(("dp", "fsdp"), None, None)
    vec = P("fsdp")
    mat = P("fsdp", None)
    in_specs = (act, vec, vec, mat, vec, vec, mat, vec, vec, vec, mat, vec, mat, vec, act)
    out_specs = (act,) + in_specs[:1] + in_specs[1:14]
    return jax.shard_map(
        lambda *a: body(n_dp, n_fsdp, *a),
        mesh=mesh,
        in_specs=in_specs,
        out_specs=out_specs,
        check_vma=False,
    )
```

```python
import math

import jax
import jax.numpy as jnp
from jax import lax
from jax.experimental import pallas as pl
from jax.experimental.pallas import tpu as pltpu
from jax.sharding import PartitionSpec as P


HEAD_DIM = 64
LANES = 128
EPS = 1e-06
F32 = jnp.float32
BF16 = jnp.bfloat16
MIB = 1 << 20


def split(v):
    hi = v.astype(BF16)
    lo = (v - hi.astype(F32)).astype(BF16)
    return hi, lo


def dot(a, b, ca, cb):
    return lax.dot_general(a, b, (((ca,), (cb,)), ((), ())), preferred_element_type=F32)


def dot3(a, b, ca, cb):
    ah, al = a
    bh, bl = b
    return dot(ah, bh, ca, cb) + (dot(ah, bl, ca, cb) + dot(al, bh, ca, cb))


def row_sum(v):
    return jnp.sum(v, axis=0, keepdims=True)


def norm_parts(v):
    center = v - jnp.mean(v, axis=-1, keepdims=True)
    inv = lax.rsqrt(jnp.mean(center * center, axis=-1, keepdims=True) + EPS)
    return center * inv, inv


def norm_back(dh, n, inv, gain):
    s = dh * gain
    return inv * (
        s - jnp.mean(s, axis=-1, keepdims=True) - n * jnp.mean(s * n, axis=-1, keepdims=True)
    )


def load_weight(offs, k, pieces, hi_ref, lo_ref):
    for p in pieces:
        at = pl.multiple_of(offs[k], 16)
        hi, lo = split(p[...])
        hi_ref[pl.ds(at, p.shape[0]), :] = hi
        lo_ref[pl.ds(at, p.shape[0]), :] = lo
        k += 1
    return k


def load_rows(offs, k, pieces, ref):
    n = ref.shape[0] // 3
    for p in pieces:
        hi, lo = split(p[...])
        for base, part in ((0, hi), (n, hi), (2 * n, lo)):
            ref[pl.ds(pl.multiple_of(base + offs[k], 16), p.shape[0]), :] = part
        k += 1


def load_cols(offs, k, pieces, ref):
    n = ref.shape[1] // 3
    for p in pieces:
        at = pl.ds(pl.multiple_of(offs[k], 16), p.shape[0])
        hi, lo = split(p[...])
        ref[at, :n] = hi
        ref[at, n : 2 * n] = hi
        ref[at, 2 * n :] = lo
        k += 1


def tall(v):
    hi, lo = split(v)
    return jnp.concatenate([hi, lo, hi], axis=1)


def fold(t):
    n = t.shape[1] // 2
    return t[:, :n] + t[:, n:]


def dot_rows(v, w3):
    hi, lo = split(v)
    n = w3.shape[0] // 3
    return fold(dot(hi, w3[n:], 1, 1)) + dot(lo, w3[:n], 1, 1)


def dot_outer(v3, w):
    n = v3.shape[1] // 3
    t = dot(v3[:, : 2 * n], w[0], 0, 0)
    return t[:n] + (t[n:] + dot(v3[:, :n], w[1], 0, 0))


def both(hi_ref, lo_ref):
    return hi_ref[...], lo_ref[...]


def lane_lt(shape):
    return lax.broadcasted_iota(jnp.int32, shape, 1) < HEAD_DIM


def swap(v):
    return pltpu.roll(v, HEAD_DIM, 1)


def pair_left(v, low):
    hi = v.astype(BF16).astype(F32)
    lo = v - hi
    zero = jnp.zeros_like(v)
    h0 = jnp.concatenate([jnp.where(low, hi, swap(lo)), jnp.where(low, hi, zero)], axis=1)
    h1 = jnp.concatenate([jnp.where(low, swap(lo), hi), jnp.where(low, zero, hi)], axis=1)
    return h0.astype(BF16), h1.astype(BF16)


def pair_right(v, low):
    hi = v.astype(BF16).astype(F32)
    lo = v - hi
    rolled = swap(hi)
    h0 = jnp.concatenate([jnp.where(low, hi, rolled), lo], axis=1)
    h1 = jnp.concatenate([jnp.where(low, rolled, hi), lo], axis=1)
    return h0.astype(BF16), h1.astype(BF16)


def wide(v):
    hi, lo = split(v)
    return hi, jnp.concatenate([hi, lo], axis=1)


def dot_wide(ph, pl_, w, ca):
    hi, cat = w
    t = dot(ph, cat, ca, 0)
    return t[:, :LANES] + (t[:, LANES:] + dot(pl_, hi, ca, 0))


def part_rows(g_ref, send_ref, keep_ref, core):
    n, rows, cols = keep_ref.shape
    for i in range(n):
        lanes = slice(i * cols, (i + 1) * cols)
        send_ref[i] = g_ref[pl.ds(pl.multiple_of((1 - core) * rows, 8), rows), lanes]
        keep_ref[i] = g_ref[pl.ds(pl.multiple_of(core * rows, 8), rows), lanes]


def part_cols(g_ref, send_ref, keep_ref, core, group=0):
    n, rows, cols = keep_ref.shape
    half = g_ref.shape[1] // 2
    for i in range(n):
        at = pl.multiple_of((1 - core) * half + group * cols, LANES)
        send_ref[i] = g_ref[i * rows : (i + 1) * rows, pl.ds(at, cols)]
        at = pl.multiple_of(core * half + group * cols, LANES)
        keep_ref[i] = g_ref[i * rows : (i + 1) * rows, pl.ds(at, cols)]


def last():
    return pl.program_id(0) == pl.num_programs(0) - 1


def first():
    return pl.program_id(0) == 0


def qkv_kernel(np_, offs, x_ref, vec_ref, *refs):
    w_pieces = refs[:np_]
    qkv_ref, w3 = refs[np_:]

    @pl.when(first())
    def _():
        load_rows(offs, 0, w_pieces, w3)

    d = x_ref.shape[2]
    vec = vec_ref[...]
    n1, _ = norm_parts(x_ref[0])
    h1 = n1 * vec[0:1] + vec[1:2]
    qkv = dot(tall(h1), w3[...], 1, 0)
    qkv_ref[0, :, :d] = qkv[:, :d] + vec[2:3]
    qkv_ref[0, :, d : 2 * d] = qkv[:, d : 2 * d]
    qkv_ref[0, :, 2 * d :] = qkv[:, 2 * d :] + vec[3:4]


def attn_fwd_kernel(offs, qkv_ref, ctx_ref, ph_ref, pl_ref):
    d = ctx_ref.shape[2]
    low = lane_lt((qkv_ref.shape[1], LANES))
    for j in range(d // LANES):
        sl = slice(j * LANES, (j + 1) * LANES)
        q = qkv_ref[0, :, sl] * (1.0 / math.sqrt(HEAD_DIM))
        k = qkv_ref[0, :, d + j * LANES : d + (j + 1) * LANES]
        v = qkv_ref[0, :, 2 * d + j * LANES : 2 * d + (j + 1) * LANES]
        qs = pair_left(q, low)
        ks = pair_right(k, low)
        vw = wide(v)
        outs = []
        for i in range(2):
            s = dot(qs[i], ks[i], 1, 1)
            e = jnp.exp(s - jnp.max(s, axis=-1, keepdims=True))
            p = e * (1.0 / jnp.sum(e, axis=-1, keepdims=True))
            hi, lo = split(p)
            ph_ref[0, 2 * j + i] = hi
            pl_ref[0, 2 * j + i] = lo
            outs.append(dot_wide(hi, lo, vw, 1))
        ctx_ref[0, :, sl] = jnp.where(low, outs[0], outs[1])


def fill_rows(buf_ref, ref):
    n, s, _ = ref.shape
    step = buf_ref.shape[0] // n
    buf_ref[...] = jnp.zeros_like(buf_ref)
    for i in range(n):
        buf_ref[i * step : i * step + s, :] = ref[i]


def take_rows(ref, rows_ref):
    n, s, _ = ref.shape
    step = rows_ref.shape[0] // n
    for i in range(n):
        ref[i] = rows_ref[i * step : i * step + s, :]


def mlp_kernel(np_, offs, x_ref, ctx_ref, dy_ref, vec_ref, b1_ref, wp, w1, *refs):
    n, n2 = np_
    pp, p1, p2 = refs[:n], refs[n : 2 * n], refs[2 * n : 2 * n + n2]
    refs = refs[2 * n + n2 :]
    out_ref, mid_ref, dh2_ref, gb1_ref, gb2_ref = refs[:5]
    send2_ref, keep2_ref, send1_ref, keep1_ref = refs[5:9]
    wph, wpl, w1r, w2c, h3, y3, mids, outs, dh2s, g2_ref, g1_ref = refs[9:]
    i = pl.program_id(0)
    d = x_ref.shape[2]
    cols = b1_ref.shape[1]
    at = pl.ds(pl.multiple_of(i * cols, LANES), cols)

    @pl.when(first())
    def _():
        vec = vec_ref[...]
        load_weight(offs, 0, [wp, *pp], wph, wpl)
        load_cols(offs, n + 1, p2, w2c)
        fill_rows(outs, ctx_ref)
        fill_rows(mids, x_ref)
        mid = mids[...] + dot3(split(outs[...]), both(wph, wpl), 1, 0) + vec[4:5]
        mids[...] = mid
        n2, _ = norm_parts(mid)
        h3[...] = tall(n2 * vec[5:6] + vec[6:7])
        fill_rows(dh2s, dy_ref)
        dy = dh2s[...]
        y3[...] = tall(dy)
        gb2_ref[...] = row_sum(dy)
        outs[...] = mid + vec[7:8]
        dh2s[...] = jnp.zeros_like(dh2s)

    load_rows(offs, 0, [w1, *p1], w1r)
    pre = dot(h3[...], w1r[...], 1, 0) + b1_ref[...]
    half = 0.5 * (1.0 + lax.erf(pre * (1.0 / math.sqrt(2.0))))
    act = split(pre * half)
    slope = half + pre * jnp.exp(-0.5 * pre * pre) * (1.0 / math.sqrt(2.0 * math.pi))
    outs[...] += fold(dot(act[0], w2c[at, d:], 1, 0)) + dot(act[1], w2c[at, :d], 1, 0)
    g2_ref[:, at] = dot_outer(y3[...], act)
    dpre = dot(y3[...], w2c[at, :], 1, 1) * slope
    gb1_ref[...] = row_sum(dpre)
    dh2s[...] += dot_rows(dpre, w1r[...])
    g1_ref[:, at] = dot_outer(h3[...], split(dpre))

    @pl.when(last())
    def _():
        take_rows(out_ref, outs)
        take_rows(mid_ref, mids)
        take_rows(dh2_ref, dh2s)
        core = offs[n + 1 + len(p2)]
        part_rows(g2_ref, send2_ref, keep2_ref, core)
        part_cols(g1_ref, send1_ref, keep1_ref, core)


def mid_kernel(np_, offs, dh2_ref, ctx_ref, dy_ref, mid_ref, vec_ref, *refs):
    gp_ref, gv_ref, dmid_ref, dctx_ref, wph, wpl = refs[np_:]

    @pl.when(first())
    def _():
        load_weight(offs, 0, refs[:np_], wph, wpl)
        gp_ref[...] = jnp.zeros_like(gp_ref)
        gv_ref[...] = jnp.zeros_like(gv_ref)

    n2, inv2 = norm_parts(mid_ref[0])
    dh2 = dh2_ref[0]
    dmid = dy_ref[0] + norm_back(dh2, n2, inv2, vec_ref[5:6])
    dmid_ref[0] = dmid
    gv_ref[0:1] += row_sum(dmid)
    gv_ref[1:2] += row_sum(dh2 * n2)
    gv_ref[2:3] += row_sum(dh2)
    dmid = split(dmid)
    gp_ref[...] += dot3(split(ctx_ref[0]), dmid, 0, 0)
    dctx_ref[0] = dot3(dmid, both(wph, wpl), 1, 1)


def attn_bwd_kernel(
    offs, x_ref, qkv_ref, ph_ref, pl_ref, ctx_ref, dctx_ref, vec_ref, gp_ref, *refs
):
    dj_ref, send0_ref, keep0_ref, send1_ref, keep1_ref, g_ref = refs
    d = ctx_ref.shape[2]

    @pl.when(first())
    def _():
        g_ref[:, : 3 * d] = jnp.zeros((d, 3 * d), F32)
        g_ref[:, 3 * d :] = gp_ref[...]

    scale = 1.0 / math.sqrt(HEAD_DIM)
    low = lane_lt((ctx_ref.shape[1], LANES))
    for j in range(d // LANES):
        sl = slice(j * LANES, (j + 1) * LANES)
        q = qkv_ref[0, :, j * LANES : (j + 1) * LANES] * scale
        k = qkv_ref[0, :, d + j * LANES : d + (j + 1) * LANES]
        v = qkv_ref[0, :, 2 * d + j * LANES : 2 * d + (j + 1) * LANES]
        dc = dctx_ref[0, :, sl]
        prod = dc * ctx_ref[0, :, sl]
        delta0 = jnp.sum(jnp.where(low, prod, 0.0), axis=-1, keepdims=True)
        delta1 = jnp.sum(jnp.where(low, 0.0, prod), axis=-1, keepdims=True)
        deltas = (delta0, delta1)
        dcs = pair_left(dc, low)
        vs = pair_right(v, low)
        qw, kw, dcw = wide(q), wide(k), wide(dc)
        dq, dk, dv = [], [], []
        for i in range(2):
            ph = ph_ref[0, 2 * j + i]
            p_lo = pl_ref[0, 2 * j + i]
            dp = dot(dcs[i], vs[i], 1, 1)
            ds = (ph.astype(F32) + p_lo.astype(F32)) * (dp - deltas[i])
            dsh, dsl = split(ds)
            dv.append(dot_wide(ph, p_lo, dcw, 0))
            dq.append(dot_wide(dsh, dsl, kw, 1))
            dk.append(dot_wide(dsh, dsl, qw, 0))
        dj_ref[0, :, sl] = jnp.where(low, dq[0], dq[1]) * scale
        dj_ref[0, :, d + j * LANES : d + (j + 1) * LANES] = jnp.where(low, dk[0], dk[1])
        dj_ref[0, :, 2 * d + j * LANES : 2 * d + (j + 1) * LANES] = jnp.where(low, dv[0], dv[1])
    n1, _ = norm_parts(x_ref[0])
    h1 = n1 * vec_ref[0:1] + vec_ref[1:2]
    g_ref[:, : 3 * d] += dot_outer(tall(h1), split(dj_ref[0]))

    @pl.when(last())
    def _():
        part_cols(g_ref, send0_ref, keep0_ref, offs[0], 0)
        part_cols(g_ref, send1_ref, keep1_ref, offs[0], 1)


def input_grad_kernel(np_, offs, x_ref, dj_ref, dmid_ref, vec_ref, *refs):
    w_pieces = refs[:np_]
    gva_ref, gb1_ref, gb2_ref = refs[np_ : np_ + 3]
    gs_ref, dx_ref, w3, gv_ref = refs[np_ + 3 :]

    @pl.when(first())
    def _():
        load_rows(offs, 0, w_pieces, w3)
        gv_ref[...] = jnp.zeros_like(gv_ref)

    d = x_ref.shape[2]
    n1, inv1 = norm_parts(x_ref[0])
    dj = dj_ref[0]
    sums = row_sum(dj)
    gv_ref[2:3] += sums[:, :d]
    gv_ref[3:4] += sums[:, 2 * d :]
    dh1 = dot_rows(dj, w3[...])
    gv_ref[0:1] += row_sum(dh1 * n1)
    gv_ref[1:2] += row_sum(dh1)
    dx_ref[0] = dmid_ref[0] + norm_back(dh1, n1, inv1, vec_ref[0:1])

    @pl.when(last())
    def _():
        shards, _, w = gs_ref.shape
        per = gb1_ref.shape[1] // (shards * w)
        for h in range(shards):
            sl = slice(h * w, (h + 1) * w)
            gs_ref[h, 0:4] = gv_ref[0:4, sl]
            gs_ref[h, 4:7] = gva_ref[0:3, sl]
            gs_ref[h, 7:8] = gb2_ref[:, sl]
            for j in range(per):
                at = (h * per + j) * w
                gs_ref[h, 8 + j : 9 + j] = gb1_ref[:, at : at + w]


def per_image(shape):
    n = len(shape)
    return pl.BlockSpec((1,) + tuple(shape[1:]), lambda i, offs: (i,) + (0,) * (n - 1))


def fixed(shape):
    n = len(shape)
    return pl.BlockSpec(tuple(shape), lambda i, offs: (0,) * n)


def block_at(shape, col):
    return pl.BlockSpec(shape, lambda i, offs: (0, col))


def run(kernel, offs, images, consts, outs, scratch, flops, blocks={}, vmem=12):
    count = images[0].shape[0]
    in_specs = [per_image(a.shape) for a in images] + [
        block_at(*blocks[i]) if i in blocks else fixed(a.shape) for i, a in enumerate(consts)
    ]
    out_specs = [per_image(s) if im else fixed(s) for s, _, im in outs]
    return pl.pallas_call(
        kernel,
        out_shape=[jax.ShapeDtypeStruct(s, t) for s, t, _ in outs],
        grid_spec=pltpu.PrefetchScalarGridSpec(
            num_scalar_prefetch=1,
            grid=(count,),
            in_specs=in_specs,
            out_specs=out_specs,
            scratch_shapes=scratch,
        ),
        cost_estimate=pl.CostEstimate(flops=flops, transcendentals=0, bytes_accessed=8 << 20),
        compiler_params=pltpu.CompilerParams(
            dimension_semantics=("arbitrary",), vmem_limit_bytes=vmem * MIB
        ),
    )(offs, *images, *consts)


def pair_scratch(rows, cols):
    return [pltpu.VMEM((rows, cols), BF16), pltpu.VMEM((rows, cols), BF16)]


def image(*shape, dtype=F32):
    return (shape, dtype, True)


def const(*shape):
    return (shape, F32, False)


def qkv_call(x, vec, w):
    offs, pieces = w
    b, s, d = x.shape
    return run(
        lambda *r: qkv_kernel(len(pieces), *r),
        offs,
        [x],
        [vec, *pieces],
        [image(b, s, 3 * d)],
        [pltpu.VMEM((3 * d, 3 * d), BF16)],
        18 * b * s * d * d,
    )[0]


def attn_fwd(qkv, zero):
    b, s, d = qkv.shape
    d = d // 3
    heads = d // HEAD_DIM
    probs = image(b, heads, s, s, dtype=BF16)
    return run(
        attn_fwd_kernel, zero, [qkv], [], [image(b, s, d), probs, probs], [],
        30 * b * s * d * d,
    )


def cols_block(shape, cols, at):
    return pl.BlockSpec((shape[0], cols), lambda i, offs: (0, at(i)))


def mlp(x, ctx, dy, vec, b1, joint, w2, core, shards):
    offs, (wp, w1, *pieces) = joint
    b, s, d = x.shape
    ff = b1.shape[1]
    rows = b * (-(-s // 8) * 8)
    c = ff // 3
    half2, half1 = (shards, d // 2, ff // shards), (shards, d // shards, ff // 2)
    shapes = [(b, s, d), (b, s, d), (b, s, d), (1, ff), (1, d), half2, half2, half1, half1]
    n = len(pieces)
    specs = [fixed(a.shape) for a in (x, ctx, dy, vec)]
    specs += [cols_block(b1.shape, c, lambda i: i), fixed(wp.shape)]
    specs += [cols_block(w1.shape, c, lambda i: i)]
    specs += [cols_block(p.shape, d, lambda i: ff // d) for p in pieces]
    specs += [cols_block(p.shape, c, lambda i: i) for p in pieces]
    specs += [fixed(p.shape) for p in w2[1]]
    out_specs = [fixed(t) for t in shapes]
    out_specs[3] = cols_block((1, ff), c, lambda i: i)
    big = pltpu.VMEM((rows, d), F32)
    tall_one = pltpu.VMEM((rows, 3 * d), BF16)
    return pl.pallas_call(
        lambda *r: mlp_kernel((n, len(w2[1])), *r),
        name="mlp",
        out_shape=[jax.ShapeDtypeStruct(t, F32) for t in shapes],
        grid_spec=pltpu.PrefetchScalarGridSpec(
            num_scalar_prefetch=1,
            grid=(ff // c,),
            in_specs=specs,
            out_specs=out_specs,
            scratch_shapes=pair_scratch(d, d)
            + [pltpu.VMEM((3 * d, c), BF16), pltpu.VMEM((ff, 3 * d), BF16)]
            + [tall_one, tall_one, big, big, big]
            + [pltpu.VMEM((d, ff), F32)] * 2,
        ),
        cost_estimate=pl.CostEstimate(
            flops=40 * b * s * d * ff, transcendentals=0, bytes_accessed=8 << 20
        ),
        compiler_params=pltpu.CompilerParams(
            dimension_semantics=("arbitrary",), vmem_limit_bytes=56 * MIB
        ),
    )(
        jnp.concatenate([offs, w2[0], core]),
        *(x, ctx, dy, vec, b1, wp, w1),
        *pieces,
        *pieces,
        *w2[1],
    )


def mlp_mid(dh2, ctx, dy, mid, vec, joint):
    offs, (wp, _, *pieces) = joint
    b, s, d = mid.shape
    return run(
        lambda *r: mid_kernel(1 + len(pieces), *r),
        offs,
        [dh2, ctx, dy, mid],
        [vec, wp, *pieces],
        [const(d, d), const(8, d), image(b, s, d), image(b, s, d)],
        pair_scratch(d, d),
        12 * b * s * d * d,
        {2 + i: ((p.shape[0], d), p.shape[1] // d - 1) for i, p in enumerate(pieces)},
        vmem=56,
    )


def attn_bwd(x, qkv, ph, p_lo, ctx, dctx, vec, gwp, core, shards):
    b, s, d = ctx.shape
    part = const(shards, d // shards, d)
    return run(
        attn_bwd_kernel,
        core,
        [x, qkv, ph, p_lo, ctx, dctx],
        [vec, gwp],
        [image(b, s, 3 * d), part, part, part, part],
        [pltpu.VMEM((d, 4 * d), F32)],
        60 * b * s * d * d,
        vmem=40,
    )


def input_grad(x, dj, dmid, vec, w, gva, gb1, gb2, shards):
    offs, pieces = w
    b, s, d = x.shape
    rows = 8 + gb1.shape[1] // d
    return run(
        lambda *r: input_grad_kernel(len(pieces), *r),
        offs,
        [x, dj, dmid],
        [vec, *pieces, gva, gb1, gb2],
        [const(shards, rows, d // shards), image(b, s, d)],
        [pltpu.VMEM((3 * d, 3 * d), BF16), pltpu.VMEM((8, d), F32)],
        18 * b * s * d * d,
    )


def tie(v, *after):
    return lax.optimization_barrier((v, *after))[0]


def ints(*values):
    return jnp.stack([jnp.asarray(v, jnp.int32) for v in values])


def swap_with(v, n_dp, n_fsdp, dp_bits, fsdp_bits):
    perm = []
    for i in range(n_dp * n_fsdp):
        d, f = divmod(i, n_fsdp)
        perm.append((i, (d ^ dp_bits) * n_fsdp + (f ^ fsdp_bits)))
    return lax.ppermute(v, ("dp", "fsdp"), perm)


class Pairs:
    def __init__(self, n_dp):
        self.n_dp, self.nz = n_dp, n_dp // 4
        self.bits = self.nz.bit_length() - 1
        dp = lax.axis_index("dp")
        self.core, self.x, self.z = dp % 2, (dp // 2) % 2, dp // 4
        self.y = lax.axis_index("fsdp")

    def over_core(self, v):
        return swap_with(v, self.n_dp, 2, 1, 0)

    def over_x(self, v):
        return swap_with(v, self.n_dp, 2, 2, 0)

    def over_y(self, v):
        return swap_with(v, self.n_dp, 2, 0, 1)

    def over_z(self, v, k):
        return swap_with(v, self.n_dp, 2, 4 * k, 0)

    def quarter(self, w, side):
        rows = w.shape[0] // 4
        return lax.dynamic_slice_in_dim(w, (2 * self.core + side) * rows, rows, 0)

    def quarter_offs(self, rows, side):
        base = (1 - self.y) * rows
        q = rows // 4
        order = [(c, i) for c in (self.core, 1 - self.core) for i in (side, 1 - side)]
        return ints(self.y * rows, *(base + (2 * c + i) * q for c, i in order))

    def finish(self, a, over):
        b = over(a)
        return [a, b, self.over_core(a), self.over_core(b)]

    def halve(self, axis, at, got, keep):
        both = [pick(got, i, axis) + pick(keep, i, axis) for i in (1 - at, at)]
        return both[0], both[1]

    def halve_x(self, got, keep):
        shape = keep.shape
        shape = shape[:-2] + (2, shape[-2] // 2, shape[-1])
        return self.halve(len(shape) - 3, self.x, got.reshape(shape), keep.reshape(shape))

    def halve_z(self, bit, got, keep):
        shape = keep.shape
        shape = shape[:-3] + (shape[-3] // 2, 2) + shape[-2:]
        at = (self.z // (1 << bit)) % 2
        return self.halve(len(shape) - 3, at, got.reshape(shape), keep.reshape(shape))

    def reduce_z(self, got, keep):
        shape = keep.shape
        shape = shape[:-2] + (self.nz, shape[-2] // self.nz, shape[-1])
        got, keep = got.reshape(shape), keep.reshape(shape)
        for bit in range(self.bits):
            send, keep = self.halve_z(bit, got, keep)
            got = self.over_z(send, 1 << bit)
        total = got + keep
        return total.reshape(total.shape[:-3] + total.shape[-2:])

    def all_reduce_z(self, v):
        for bit in range(self.bits):
            v = v + self.over_z(v, 1 << bit)
        return v

    def gather(self, v):
        high = list(range(self.bits))[:0:-1]
        for bit in high[:-1]:
            v = jnp.stack([v, self.over_z(v, 1 << bit)])
        if high:
            got = self.over_z(v, 1 << high[-1])
            two = [jnp.stack([v[..., i, :, :], got[..., i, :, :]]) for i in range(2)]
        else:
            two = [v[..., i, :, :] for i in range(2)]
        two = [t.reshape((-1,) + t.shape[-2:]) for t in two]
        got0 = self.over_x(two[0])
        got1 = self.over_z(two[1], 1)
        two = [jnp.concatenate([two[0], got0]), jnp.concatenate([two[1], got1])]
        got0 = self.over_z(two[0], 1)
        got1 = self.over_x(two[1])
        stacks = [two[0], got0, two[1], got1]
        stacks = stacks + [self.over_core(t) for t in stacks]
        base = self.placed(high, False)
        moves = []
        for dc in range(2):
            group0 = [(0, dc, dx, dz) for dx in range(2) for _, dz in base]
            group1 = [(1, dc, 0, dz ^ low) for low in range(2) for _, dz in base]
            moves += [group0, [(g, c, dx, dz ^ 1) for g, c, dx, dz in group0]]
            moves += [group1, [(g, c, 1 - dx, dz) for g, c, dx, dz in group1]]
        return stacks, moves

    def placed(self, bits, with_x):
        out = []
        names = list(bits) + (["x"] if with_x else [])
        for i in range(1 << len(names)):
            at = [(i >> k) & 1 for k in range(len(names))]
            dz = sum(a << n for a, n in zip(at, names) if n != "x")
            dx = sum(a for a, n in zip(at, names) if n == "x")
            out.append((dx, dz))
        return out

    def join(self, stacks, moves, put, outs, scratch=(), finish=None):
        nz = self.nz
        n_out = len(outs)

        def kernel(pos, *refs):
            ins, refs = refs[: len(stacks)], refs[len(stacks) :]
            for core in range(2):

                @pl.when(pos[0] == core)
                def _():
                    for ref, places in zip(ins, moves):
                        for k, (group, dc, dx, dz) in enumerate(places):
                            row = (pos[1] ^ dx) * nz + (pos[2] ^ dz)
                            put(ref.at[k], group, core ^ dc, row, refs)

            if finish is not None:
                finish(refs)

        return pl.pallas_call(
            kernel,
            out_shape=[jax.ShapeDtypeStruct(s, F32) for s in outs],
            grid_spec=pltpu.PrefetchScalarGridSpec(
                num_scalar_prefetch=1,
                grid=(1,),
                in_specs=[fixed(a.shape) for a in stacks],
                out_specs=[fixed(s) for s in outs],
                scratch_shapes=list(scratch),
            ),
            compiler_params=pltpu.CompilerParams(vmem_limit_bytes=8 * MIB),
        )(ints(self.core, self.x, self.z), *stacks)

    def join_attn(self, stacks, moves, d):
        r = stacks[0].shape[1]
        rows = 2 * self.nz * r

        def put(ref, group, core, row, refs):
            at = pl.ds(pl.multiple_of(row * r, 8), r)
            k = 2 * core + group
            if k < 3:
                refs[0][at, k * d : (k + 1) * d] = ref[...]
            else:
                refs[1][at, :] = ref[...]

        return self.join(stacks, moves, put, [(rows, 3 * d), (rows, d)])

    def join_mlp(self, stacks, moves):
        _, r, cols = stacks[0].shape
        rows = 2 * self.nz * r

        def put(ref, group, core, row, refs):
            at = pl.multiple_of(row * r, 8)
            if group == 0:
                refs[2][pl.ds(core * rows + at, r), :] = ref[...]
            else:
                refs[1][pl.ds(at, r), core * cols : (core + 1) * cols] = ref[...]

        def finish(refs):
            refs[0][...] = refs[2][...].T

        outs = [(cols, 2 * rows), (rows, 2 * cols)]
        scratch = [pltpu.VMEM((2 * rows, cols), F32)]
        return self.join(stacks, moves, put, outs, scratch, finish)


def pick(v, i, axis=0):
    return lax.dynamic_index_in_dim(v, i, axis, keepdims=False)


def whole_mesh_step(n_fsdp, x, vec, b1f, wqkv, wproj, wfc1, wfc2, dy):
    def gather(w):
        return lax.all_gather(w, "fsdp", axis=0, tiled=True)

    def total(v):
        part = lax.psum_scatter(v, "fsdp", scatter_dimension=0, tiled=True)
        return lax.psum(part, "dp")[0]

    zero = ints(0)
    d = x.shape[2]
    w_qkv, w_2 = (zero, [gather(wqkv)]), (zero, [gather(wfc2)])
    joint = zero, [gather(wproj), gather(wfc1)]
    qkv = qkv_call(x, vec, w_qkv)
    ctx, ph, p_lo = attn_fwd(qkv, zero)
    out, mid, dh2, gb1, gb2, send2, keep2, send1, keep1 = mlp(
        x, ctx, dy, vec, b1f, joint, w_2, zero, n_fsdp
    )
    gwp, gva, dmid, dctx = mlp_mid(dh2, ctx, dy, mid, vec, joint)
    dj, *parts = attn_bwd(x, qkv, ph, p_lo, ctx, dctx, vec, gwp, zero, n_fsdp)
    gs, dx = input_grad(x, dj, dmid, vec, w_qkv, gva, gb1, gb2, n_fsdp)
    ga = jnp.concatenate([total(parts[i]) for i in (1, 3, 0, 2)], axis=1)
    gw1 = jnp.concatenate([total(keep1), total(send1)], axis=1)
    gw2 = jnp.concatenate([total(keep2), total(send2)], axis=0).T
    return out, dx, ga[:, : 3 * d], ga[:, 3 * d :], gw1, gw2, small_grads(total(gs))


def pair_step(n_dp, x, vec, b1f, wqkv, wproj, wfc1, wfc2, dy):
    c = Pairs(n_dp)
    core = ints(c.core)
    d = x.shape[2]
    z0 = c.z % 2
    came = c.over_y(c.quarter(wqkv, c.x))
    w_qkv = c.quarter_offs(wqkv.shape[0], c.x), [wqkv, *c.finish(came, c.over_x)]
    joint = [c.quarter(wfc1, c.x), c.quarter(wproj, c.x)]
    joint = c.over_y(jnp.concatenate(joint, axis=1))
    w_2 = c.over_y(c.quarter(wfc2, z0))
    qkv = qkv_call(x, vec, w_qkv)
    pieces = c.finish(tie(joint, qkv), c.over_x)
    joint = c.quarter_offs(wproj.shape[0], c.x), [wproj, wfc1, *pieces]
    ctx, ph, p_lo = attn_fwd(qkv, core)
    pieces = c.finish(tie(w_2, qkv), lambda v: c.over_z(v, 1))
    w_2 = c.quarter_offs(wfc2.shape[0], z0), [wfc2, *pieces]
    out, mid, dh2, gb1, gb2, send2, keep2, send1, keep1 = mlp(
        x, ctx, dy, vec, b1f, joint, w_2, core, 2
    )
    got2 = c.over_core(send2)
    got1 = c.over_core(send1)
    gwp, gva, dmid, dctx = mlp_mid(dh2, ctx, dy, mid, vec, joint)
    send2, keep2 = c.halve_x(got2, keep2)
    send1, keep1 = c.halve(0, c.y, got1, keep1)
    got2 = c.over_x(send2)
    got1 = c.over_y(send1)
    dctx = tie(dctx, send1, keep1, send2, keep2)
    dj, send3, keep3, send4, keep4 = attn_bwd(x, qkv, ph, p_lo, ctx, dctx, vec, gwp, core, 2)
    got3 = c.over_core(send3)
    got4 = c.over_core(send4)
    send2, keep2 = c.halve(0, c.y, got2, keep2)
    send1, keep1 = c.halve_x(got1, keep1)
    got2 = c.over_y(send2)
    got1 = c.over_x(send1)
    dj = tie(dj, send3, send4, send1, keep1, send2, keep2)
    gs, dx = input_grad(x, dj, dmid, vec, w_qkv, gva, gb1, gb2, 2)
    send3, keep3 = c.halve_x(got3, keep3)
    send4, keep4 = c.halve(0, c.y, got4, keep4)
    got3 = c.over_x(send3)
    got4 = c.over_y(send4)
    gs = gs + c.over_core(tie(gs, send3, send4))
    gs_y = c.over_y(pick(gs, 1 - c.y))
    gs = pick(gs, c.y) + gs_y
    gs_x = c.over_x(gs)
    gotf, keepf = jnp.stack([got2, got1]), jnp.stack([keep2, keep1])
    f = c.reduce_z(gotf, keepf)
    f, moves_f = c.gather(f)
    send3, keep3 = c.halve(0, c.y, got3, keep3)
    send4, keep4 = c.halve_x(got4, keep4)
    got3 = c.over_y(send3)
    got4 = c.over_x(send4)
    gota, keepa = jnp.stack([got3, got4]), jnp.stack([keep3, keep4])
    a = c.reduce_z(gota, keepa)
    gs = c.all_reduce_z(gs + gs_x)
    a, moves_a = c.gather(a)
    gw2, gw1 = c.join_mlp(f, moves_f)
    gwqkv, gwproj = c.join_attn(a, moves_a, d)
    return out, dx, gwqkv, gwproj, gw1, gw2, small_grads(gs)


def small_grads(gs):
    return [*(gs[i] for i in range(8)), gs[8:].reshape(-1)]


def is_pairs(n_dp, n_fsdp):
    return n_fsdp == 2 and n_dp >= 8 and (n_dp & (n_dp - 1)) == 0


def body(n_dp, n_fsdp, x, g1, s1, wqkv, qb, vb, wproj, pb, g2, s2, wfc1, b1, wfc2, b2, dy):
    pairs = is_pairs(n_dp, n_fsdp)
    w = g1.shape[0]
    small = jnp.concatenate([jnp.stack([g1, s1, qb, vb, pb, g2, s2, b2]), b1.reshape(-1, w)])
    if pairs:
        other = swap_with(small, n_dp, n_fsdp, 0, 1)
        is_first = lax.axis_index("fsdp") == 0
        small = jnp.stack([jnp.where(is_first, small, other), jnp.where(is_first, other, small)])
    else:
        small = lax.all_gather(small, "fsdp", axis=0)
    vec = small[:, :8].transpose(1, 0, 2).reshape(8, -1)
    b1f = small[:, 8:].reshape(1, -1)
    args = (x, vec, b1f, wqkv, wproj, wfc1, wfc2, dy)
    step = pair_step(n_dp, *args) if pairs else whole_mesh_step(n_fsdp, *args)
    out, dx, gwqkv, gwproj, gw1, gw2, gs = step
    return (
        out,
        dx,
        gs[0],
        gs[1],
        gwqkv,
        gs[2],
        gs[3],
        gwproj,
        gs[4],
        gs[5],
        gs[6],
        gw1,
        gs[8],
        gw2,
        gs[7],
    )


def solution(mesh):
    n_dp, n_fsdp = mesh.shape["dp"], mesh.shape["fsdp"]
    act = P(("dp", "fsdp"), None, None)
    vec = P("fsdp")
    mat = P("fsdp", None)
    in_specs = (act, vec, vec, mat, vec, vec, mat, vec, vec, vec, mat, vec, mat, vec, act)
    out_specs = (act,) + in_specs[:1] + in_specs[1:14]
    return jax.shard_map(
        lambda *a: body(n_dp, n_fsdp, *a),
        mesh=mesh,
        in_specs=in_specs,
        out_specs=out_specs,
        check_vma=False,
    )
```

```python
import math

import jax
import jax.numpy as jnp
from jax import lax
from jax.experimental import pallas as pl
from jax.experimental.pallas import tpu as pltpu
from jax.sharding import PartitionSpec as P


HEAD_DIM = 64
LANES = 128
EPS = 1e-06
F32 = jnp.float32
BF16 = jnp.bfloat16
MIB = 1 << 20


def split(v):
    hi = v.astype(BF16)
    lo = (v - hi.astype(F32)).astype(BF16)
    return hi, lo


def dot(a, b, ca, cb):
    return lax.dot_general(a, b, (((ca,), (cb,)), ((), ())), preferred_element_type=F32)


def dot3(a, b, ca, cb):
    ah, al = a
    bh, bl = b
    return dot(ah, bh, ca, cb) + (dot(ah, bl, ca, cb) + dot(al, bh, ca, cb))


def row_sum(v):
    return jnp.sum(v, axis=0, keepdims=True)


def norm_parts(v):
    center = v - jnp.mean(v, axis=-1, keepdims=True)
    inv = lax.rsqrt(jnp.mean(center * center, axis=-1, keepdims=True) + EPS)
    return center * inv, inv


def norm_back(dh, n, inv, gain):
    s = dh * gain
    return inv * (
        s - jnp.mean(s, axis=-1, keepdims=True) - n * jnp.mean(s * n, axis=-1, keepdims=True)
    )


def load_weight(offs, k, pieces, hi_ref, lo_ref):
    for p in pieces:
        at = pl.multiple_of(offs[k], 16)
        hi, lo = split(p[...])
        hi_ref[pl.ds(at, p.shape[0]), :] = hi
        lo_ref[pl.ds(at, p.shape[0]), :] = lo
        k += 1
    return k


def load_rows(offs, k, pieces, ref):
    n = ref.shape[0] // 3
    for p in pieces:
        hi, lo = split(p[...])
        for base, part in ((0, hi), (n, hi), (2 * n, lo)):
            ref[pl.ds(pl.multiple_of(base + offs[k], 16), p.shape[0]), :] = part
        k += 1


def load_cols(offs, k, pieces, ref):
    n = ref.shape[1] // 3
    for p in pieces:
        at = pl.ds(pl.multiple_of(offs[k], 16), p.shape[0])
        hi, lo = split(p[...])
        ref[at, :n] = hi
        ref[at, n : 2 * n] = hi
        ref[at, 2 * n :] = lo
        k += 1


def tall(v):
    hi, lo = split(v)
    return jnp.concatenate([hi, lo, hi], axis=1)


def fold(t):
    n = t.shape[1] // 2
    return t[:, :n] + t[:, n:]


def dot_rows(v, w3):
    hi, lo = split(v)
    n = w3.shape[0] // 3
    return fold(dot(hi, w3[n:], 1, 1)) + dot(lo, w3[:n], 1, 1)


def dot_outer(v3, w):
    n = v3.shape[1] // 3
    t = dot(v3[:, : 2 * n], w[0], 0, 0)
    return t[:n] + (t[n:] + dot(v3[:, :n], w[1], 0, 0))


def both(hi_ref, lo_ref):
    return hi_ref[...], lo_ref[...]


def lane_lt(shape):
    return lax.broadcasted_iota(jnp.int32, shape, 1) < HEAD_DIM


def swap(v):
    return pltpu.roll(v, HEAD_DIM, 1)


def pair_left(v, low):
    hi = v.astype(BF16).astype(F32)
    lo = v - hi
    zero = jnp.zeros_like(v)
    h0 = jnp.concatenate([jnp.where(low, hi, swap(lo)), jnp.where(low, hi, zero)], axis=1)
    h1 = jnp.concatenate([jnp.where(low, swap(lo), hi), jnp.where(low, zero, hi)], axis=1)
    return h0.astype(BF16), h1.astype(BF16)


def pair_right(v, low):
    hi = v.astype(BF16).astype(F32)
    lo = v - hi
    rolled = swap(hi)
    h0 = jnp.concatenate([jnp.where(low, hi, rolled), lo], axis=1)
    h1 = jnp.concatenate([jnp.where(low, rolled, hi), lo], axis=1)
    return h0.astype(BF16), h1.astype(BF16)


def wide(v):
    hi, lo = split(v)
    return hi, jnp.concatenate([hi, lo], axis=1)


def dot_wide(ph, pl_, w, ca):
    hi, cat = w
    t = dot(ph, cat, ca, 0)
    return t[:, :LANES] + (t[:, LANES:] + dot(pl_, hi, ca, 0))


def part_rows(g_ref, send_ref, keep_ref, core):
    n, rows, cols = keep_ref.shape
    for i in range(n):
        lanes = slice(i * cols, (i + 1) * cols)
        send_ref[i] = g_ref[pl.ds(pl.multiple_of((1 - core) * rows, 8), rows), lanes]
        keep_ref[i] = g_ref[pl.ds(pl.multiple_of(core * rows, 8), rows), lanes]


def part_cols(g_ref, send_ref, keep_ref, core, group=0):
    n, rows, cols = keep_ref.shape
    half = g_ref.shape[1] // 2
    for i in range(n):
        at = pl.multiple_of((1 - core) * half + group * cols, LANES)
        send_ref[i] = g_ref[i * rows : (i + 1) * rows, pl.ds(at, cols)]
        at = pl.multiple_of(core * half + group * cols, LANES)
        keep_ref[i] = g_ref[i * rows : (i + 1) * rows, pl.ds(at, cols)]


def last():
    return pl.program_id(0) == pl.num_programs(0) - 1


def first():
    return pl.program_id(0) == 0


def qkv_kernel(np_, offs, x_ref, vec_ref, *refs):
    w_pieces = refs[:np_]
    qkv_ref, w3 = refs[np_:]

    @pl.when(first())
    def _():
        load_rows(offs, 0, w_pieces, w3)

    d = x_ref.shape[2]
    vec = vec_ref[...]
    n1, _ = norm_parts(x_ref[0])
    h1 = n1 * vec[0:1] + vec[1:2]
    qkv = dot(tall(h1), w3[...], 1, 0)
    qkv_ref[0, :, :d] = qkv[:, :d] + vec[2:3]
    qkv_ref[0, :, d : 2 * d] = qkv[:, d : 2 * d]
    qkv_ref[0, :, 2 * d :] = qkv[:, 2 * d :] + vec[3:4]


def attn_fwd_kernel(offs, qkv_ref, ctx_ref, ph_ref, pl_ref):
    d = ctx_ref.shape[2]
    low = lane_lt((qkv_ref.shape[1], LANES))
    for j in range(d // LANES):
        sl = slice(j * LANES, (j + 1) * LANES)
        q = qkv_ref[0, :, sl] * (1.0 / math.sqrt(HEAD_DIM))
        k = qkv_ref[0, :, d + j * LANES : d + (j + 1) * LANES]
        v = qkv_ref[0, :, 2 * d + j * LANES : 2 * d + (j + 1) * LANES]
        qs = pair_left(q, low)
        ks = pair_right(k, low)
        vw = wide(v)
        outs = []
        for i in range(2):
            s = dot(qs[i], ks[i], 1, 1)
            e = jnp.exp(s - jnp.max(s, axis=-1, keepdims=True))
            p = e * (1.0 / jnp.sum(e, axis=-1, keepdims=True))
            hi, lo = split(p)
            ph_ref[0, 2 * j + i] = hi
            pl_ref[0, 2 * j + i] = lo
            outs.append(dot_wide(hi, lo, vw, 1))
        ctx_ref[0, :, sl] = jnp.where(low, outs[0], outs[1])


def fill_rows(buf_ref, ref):
    n, s, _ = ref.shape
    step = buf_ref.shape[0] // n
    buf_ref[...] = jnp.zeros_like(buf_ref)
    for i in range(n):
        buf_ref[i * step : i * step + s, :] = ref[i]


def take_rows(ref, rows_ref):
    n, s, _ = ref.shape
    step = rows_ref.shape[0] // n
    for i in range(n):
        ref[i] = rows_ref[i * step : i * step + s, :]


def mlp_kernel(np_, offs, x_ref, ctx_ref, dy_ref, vec_ref, b1_ref, wp, w1, *refs):
    n, n2 = np_
    pp, p1, p2 = refs[:n], refs[n : 2 * n], refs[2 * n : 2 * n + n2]
    refs = refs[2 * n + n2 :]
    out_ref, mid_ref, dh2_ref, gb1_ref, gb2_ref = refs[:5]
    send2_ref, keep2_ref, send1_ref, keep1_ref = refs[5:9]
    wph, wpl, w1r, w2c, h3, y3, mids, outs, dh2s, g2_ref, g1_ref = refs[9:]
    i = pl.program_id(0)
    d = x_ref.shape[2]
    cols = b1_ref.shape[1]
    at = pl.ds(pl.multiple_of(i * cols, LANES), cols)

    @pl.when(first())
    def _():
        vec = vec_ref[...]
        load_weight(offs, 0, [wp, *pp], wph, wpl)
        load_cols(offs, n + 1, p2, w2c)
        fill_rows(outs, ctx_ref)
        fill_rows(mids, x_ref)
        mid = mids[...] + dot3(split(outs[...]), both(wph, wpl), 1, 0) + vec[4:5]
        mids[...] = mid
        n2, _ = norm_parts(mid)
        h3[...] = tall(n2 * vec[5:6] + vec[6:7])
        fill_rows(dh2s, dy_ref)
        dy = dh2s[...]
        y3[...] = tall(dy)
        gb2_ref[...] = row_sum(dy)
        outs[...] = mid + vec[7:8]
        dh2s[...] = jnp.zeros_like(dh2s)

    load_rows(offs, 0, [w1, *p1], w1r)
    pre = dot(h3[...], w1r[...], 1, 0) + b1_ref[...]
    half = 0.5 * (1.0 + lax.erf(pre * (1.0 / math.sqrt(2.0))))
    act = split(pre * half)
    slope = half + pre * jnp.exp(-0.5 * pre * pre) * (1.0 / math.sqrt(2.0 * math.pi))
    outs[...] += fold(dot(act[0], w2c[at, d:], 1, 0)) + dot(act[1], w2c[at, :d], 1, 0)
    g2_ref[:, at] = dot_outer(y3[...], act)
    dpre = dot(y3[...], w2c[at, :], 1, 1) * slope
    gb1_ref[...] = row_sum(dpre)
    dh2s[...] += dot_rows(dpre, w1r[...])
    g1_ref[:, at] = dot_outer(h3[...], split(dpre))

    @pl.when(last())
    def _():
        take_rows(out_ref, outs)
        take_rows(mid_ref, mids)
        take_rows(dh2_ref, dh2s)
        core = offs[n + 1 + len(p2)]
        part_rows(g2_ref, send2_ref, keep2_ref, core)
        part_cols(g1_ref, send1_ref, keep1_ref, core)


def mid_kernel(np_, offs, dh2_ref, ctx_ref, dy_ref, mid_ref, vec_ref, *refs):
    gp_ref, gv_ref, dmid_ref, dctx_ref, wph, wpl = refs[np_:]

    @pl.when(first())
    def _():
        load_weight(offs, 0, refs[:np_], wph, wpl)
        gp_ref[...] = jnp.zeros_like(gp_ref)
        gv_ref[...] = jnp.zeros_like(gv_ref)

    n2, inv2 = norm_parts(mid_ref[0])
    dh2 = dh2_ref[0]
    dmid = dy_ref[0] + norm_back(dh2, n2, inv2, vec_ref[5:6])
    dmid_ref[0] = dmid
    gv_ref[0:1] += row_sum(dmid)
    gv_ref[1:2] += row_sum(dh2 * n2)
    gv_ref[2:3] += row_sum(dh2)
    dmid = split(dmid)
    gp_ref[...] += dot3(split(ctx_ref[0]), dmid, 0, 0)
    dctx_ref[0] = dot3(dmid, both(wph, wpl), 1, 1)


def attn_bwd_kernel(
    offs, x_ref, qkv_ref, ph_ref, pl_ref, ctx_ref, dctx_ref, vec_ref, gp_ref, *refs
):
    dj_ref, send0_ref, keep0_ref, send1_ref, keep1_ref, g_ref = refs
    d = ctx_ref.shape[2]

    @pl.when(first())
    def _():
        g_ref[:, : 3 * d] = jnp.zeros((d, 3 * d), F32)
        g_ref[:, 3 * d :] = gp_ref[...]

    scale = 1.0 / math.sqrt(HEAD_DIM)
    low = lane_lt((ctx_ref.shape[1], LANES))
    for j in range(d // LANES):
        sl = slice(j * LANES, (j + 1) * LANES)
        q = qkv_ref[0, :, j * LANES : (j + 1) * LANES] * scale
        k = qkv_ref[0, :, d + j * LANES : d + (j + 1) * LANES]
        v = qkv_ref[0, :, 2 * d + j * LANES : 2 * d + (j + 1) * LANES]
        dc = dctx_ref[0, :, sl]
        prod = dc * ctx_ref[0, :, sl]
        delta0 = jnp.sum(jnp.where(low, prod, 0.0), axis=-1, keepdims=True)
        delta1 = jnp.sum(jnp.where(low, 0.0, prod), axis=-1, keepdims=True)
        deltas = (delta0, delta1)
        dcs = pair_left(dc, low)
        vs = pair_right(v, low)
        qw, kw, dcw = wide(q), wide(k), wide(dc)
        dq, dk, dv = [], [], []
        for i in range(2):
            ph = ph_ref[0, 2 * j + i]
            p_lo = pl_ref[0, 2 * j + i]
            dp = dot(dcs[i], vs[i], 1, 1)
            ds = (ph.astype(F32) + p_lo.astype(F32)) * (dp - deltas[i])
            dsh, dsl = split(ds)
            dv.append(dot_wide(ph, p_lo, dcw, 0))
            dq.append(dot_wide(dsh, dsl, kw, 1))
            dk.append(dot_wide(dsh, dsl, qw, 0))
        dj_ref[0, :, sl] = jnp.where(low, dq[0], dq[1]) * scale
        dj_ref[0, :, d + j * LANES : d + (j + 1) * LANES] = jnp.where(low, dk[0], dk[1])
        dj_ref[0, :, 2 * d + j * LANES : 2 * d + (j + 1) * LANES] = jnp.where(low, dv[0], dv[1])
    n1, _ = norm_parts(x_ref[0])
    h1 = n1 * vec_ref[0:1] + vec_ref[1:2]
    g_ref[:, : 3 * d] += dot_outer(tall(h1), split(dj_ref[0]))

    @pl.when(last())
    def _():
        part_cols(g_ref, send0_ref, keep0_ref, offs[0], 0)
        part_cols(g_ref, send1_ref, keep1_ref, offs[0], 1)


def input_grad_kernel(np_, offs, x_ref, dj_ref, dmid_ref, vec_ref, *refs):
    w_pieces = refs[:np_]
    gva_ref, gb1_ref, gb2_ref = refs[np_ : np_ + 3]
    gs_ref, dx_ref, w3, gv_ref = refs[np_ + 3 :]

    @pl.when(first())
    def _():
        load_rows(offs, 0, w_pieces, w3)
        gv_ref[...] = jnp.zeros_like(gv_ref)

    d = x_ref.shape[2]
    n1, inv1 = norm_parts(x_ref[0])
    dj = dj_ref[0]
    sums = row_sum(dj)
    gv_ref[2:3] += sums[:, :d]
    gv_ref[3:4] += sums[:, 2 * d :]
    dh1 = dot_rows(dj, w3[...])
    gv_ref[0:1] += row_sum(dh1 * n1)
    gv_ref[1:2] += row_sum(dh1)
    dx_ref[0] = dmid_ref[0] + norm_back(dh1, n1, inv1, vec_ref[0:1])

    @pl.when(last())
    def _():
        shards, _, w = gs_ref.shape
        per = gb1_ref.shape[1] // (shards * w)
        for h in range(shards):
            sl = slice(h * w, (h + 1) * w)
            gs_ref[h, 0:4] = gv_ref[0:4, sl]
            gs_ref[h, 4:7] = gva_ref[0:3, sl]
            gs_ref[h, 7:8] = gb2_ref[:, sl]
            for j in range(per):
                at = (h * per + j) * w
                gs_ref[h, 8 + j : 9 + j] = gb1_ref[:, at : at + w]


def per_image(shape):
    n = len(shape)
    return pl.BlockSpec((1,) + tuple(shape[1:]), lambda i, offs: (i,) + (0,) * (n - 1))


def fixed(shape):
    n = len(shape)
    return pl.BlockSpec(tuple(shape), lambda i, offs: (0,) * n)


def block_at(shape, col):
    return pl.BlockSpec(shape, lambda i, offs: (0, col))


def run(kernel, offs, images, consts, outs, scratch, flops, blocks={}, vmem=12):
    count = images[0].shape[0]
    in_specs = [per_image(a.shape) for a in images] + [
        block_at(*blocks[i]) if i in blocks else fixed(a.shape) for i, a in enumerate(consts)
    ]
    out_specs = [per_image(s) if im else fixed(s) for s, _, im in outs]
    return pl.pallas_call(
        kernel,
        out_shape=[jax.ShapeDtypeStruct(s, t) for s, t, _ in outs],
        grid_spec=pltpu.PrefetchScalarGridSpec(
            num_scalar_prefetch=1,
            grid=(count,),
            in_specs=in_specs,
            out_specs=out_specs,
            scratch_shapes=scratch,
        ),
        cost_estimate=pl.CostEstimate(flops=flops, transcendentals=0, bytes_accessed=8 << 20),
        compiler_params=pltpu.CompilerParams(
            dimension_semantics=("arbitrary",), vmem_limit_bytes=vmem * MIB
        ),
    )(offs, *images, *consts)


def pair_scratch(rows, cols):
    return [pltpu.VMEM((rows, cols), BF16), pltpu.VMEM((rows, cols), BF16)]


def image(*shape, dtype=F32):
    return (shape, dtype, True)


def const(*shape):
    return (shape, F32, False)


def qkv_call(x, vec, w):
    offs, pieces = w
    b, s, d = x.shape
    return run(
        lambda *r: qkv_kernel(len(pieces), *r),
        offs,
        [x],
        [vec, *pieces],
        [image(b, s, 3 * d)],
        [pltpu.VMEM((3 * d, 3 * d), BF16)],
        18 * b * s * d * d,
    )[0]


def attn_fwd(qkv, zero):
    b, s, d = qkv.shape
    d = d // 3
    heads = d // HEAD_DIM
    probs = image(b, heads, s, s, dtype=BF16)
    return run(
        attn_fwd_kernel, zero, [qkv], [], [image(b, s, d), probs, probs], [],
        30 * b * s * d * d, vmem=56,
    )


def cols_block(shape, cols, at):
    return pl.BlockSpec((shape[0], cols), lambda i, offs: (0, at(i)))


def mlp(x, ctx, dy, vec, b1, joint, w2, core, shards):
    offs, (wp, w1, *pieces) = joint
    b, s, d = x.shape
    ff = b1.shape[1]
    rows = b * (-(-s // 8) * 8)
    c = ff // 3
    half2, half1 = (shards, d // 2, ff // shards), (shards, d // shards, ff // 2)
    shapes = [(b, s, d), (b, s, d), (b, s, d), (1, ff), (1, d), half2, half2, half1, half1]
    n = len(pieces)
    specs = [fixed(a.shape) for a in (x, ctx, dy, vec)]
    specs += [cols_block(b1.shape, c, lambda i: i), fixed(wp.shape)]
    specs += [cols_block(w1.shape, c, lambda i: i)]
    specs += [cols_block(p.shape, d, lambda i: ff // d) for p in pieces]
    specs += [cols_block(p.shape, c, lambda i: i) for p in pieces]
    specs += [fixed(p.shape) for p in w2[1]]
    out_specs = [fixed(t) for t in shapes]
    out_specs[3] = cols_block((1, ff), c, lambda i: i)
    big = pltpu.VMEM((rows, d), F32)
    tall_one = pltpu.VMEM((rows, 3 * d), BF16)
    return pl.pallas_call(
        lambda *r: mlp_kernel((n, len(w2[1])), *r),
        name="mlp",
        out_shape=[jax.ShapeDtypeStruct(t, F32) for t in shapes],
        grid_spec=pltpu.PrefetchScalarGridSpec(
            num_scalar_prefetch=1,
            grid=(ff // c,),
            in_specs=specs,
            out_specs=out_specs,
            scratch_shapes=pair_scratch(d, d)
            + [pltpu.VMEM((3 * d, c), BF16), pltpu.VMEM((ff, 3 * d), BF16)]
            + [tall_one, tall_one, big, big, big]
            + [pltpu.VMEM((d, ff), F32)] * 2,
        ),
        cost_estimate=pl.CostEstimate(
            flops=40 * b * s * d * ff, transcendentals=0, bytes_accessed=8 << 20
        ),
        compiler_params=pltpu.CompilerParams(
            dimension_semantics=("arbitrary",), vmem_limit_bytes=56 * MIB
        ),
    )(
        jnp.concatenate([offs, w2[0], core]),
        *(x, ctx, dy, vec, b1, wp, w1),
        *pieces,
        *pieces,
        *w2[1],
    )


def mlp_mid(dh2, ctx, dy, mid, vec, joint):
    offs, (wp, _, *pieces) = joint
    b, s, d = mid.shape
    return run(
        lambda *r: mid_kernel(1 + len(pieces), *r),
        offs,
        [dh2, ctx, dy, mid],
        [vec, wp, *pieces],
        [const(d, d), const(8, d), image(b, s, d), image(b, s, d)],
        pair_scratch(d, d),
        12 * b * s * d * d,
        {2 + i: ((p.shape[0], d), p.shape[1] // d - 1) for i, p in enumerate(pieces)},
        vmem=56,
    )


def attn_bwd(x, qkv, ph, p_lo, ctx, dctx, vec, gwp, core, shards):
    b, s, d = ctx.shape
    part = const(shards, d // shards, d)
    return run(
        attn_bwd_kernel,
        core,
        [x, qkv, ph, p_lo, ctx, dctx],
        [vec, gwp],
        [image(b, s, 3 * d), part, part, part, part],
        [pltpu.VMEM((d, 4 * d), F32)],
        60 * b * s * d * d,
        vmem=40,
    )


def input_grad(x, dj, dmid, vec, w, gva, gb1, gb2, shards):
    offs, pieces = w
    b, s, d = x.shape
    rows = 8 + gb1.shape[1] // d
    return run(
        lambda *r: input_grad_kernel(len(pieces), *r),
        offs,
        [x, dj, dmid],
        [vec, *pieces, gva, gb1, gb2],
        [const(shards, rows, d // shards), image(b, s, d)],
        [pltpu.VMEM((3 * d, 3 * d), BF16), pltpu.VMEM((8, d), F32)],
        18 * b * s * d * d,
    )


def tie(v, *after):
    return lax.optimization_barrier((v, *after))[0]


def ints(*values):
    return jnp.stack([jnp.asarray(v, jnp.int32) for v in values])


def swap_with(v, n_dp, n_fsdp, dp_bits, fsdp_bits):
    perm = []
    for i in range(n_dp * n_fsdp):
        d, f = divmod(i, n_fsdp)
        perm.append((i, (d ^ dp_bits) * n_fsdp + (f ^ fsdp_bits)))
    return lax.ppermute(v, ("dp", "fsdp"), perm)


class Pairs:
    def __init__(self, n_dp):
        self.n_dp, self.nz = n_dp, n_dp // 4
        self.bits = self.nz.bit_length() - 1
        dp = lax.axis_index("dp")
        self.core, self.x, self.z = dp % 2, (dp // 2) % 2, dp // 4
        self.y = lax.axis_index("fsdp")

    def over_core(self, v):
        return swap_with(v, self.n_dp, 2, 1, 0)

    def over_x(self, v):
        return swap_with(v, self.n_dp, 2, 2, 0)

    def over_y(self, v):
        return swap_with(v, self.n_dp, 2, 0, 1)

    def over_z(self, v, k):
        return swap_with(v, self.n_dp, 2, 4 * k, 0)

    def quarter(self, w, side):
        rows = w.shape[0] // 4
        return lax.dynamic_slice_in_dim(w, (2 * self.core + side) * rows, rows, 0)

    def quarter_offs(self, rows, side):
        base = (1 - self.y) * rows
        q = rows // 4
        order = [(c, i) for c in (self.core, 1 - self.core) for i in (side, 1 - side)]
        return ints(self.y * rows, *(base + (2 * c + i) * q for c, i in order))

    def finish(self, a, over):
        b = over(a)
        return [a, b, self.over_core(a), self.over_core(b)]

    def halve(self, axis, at, terms):
        return sum(pick(t, 1 - at, axis) for t in terms), [pick(t, at, axis) for t in terms]

    def halve_y(self, terms):
        return self.halve(0, self.y, terms)

    def halve_x(self, terms):
        shape = terms[0].shape
        shape = shape[:-2] + (2, shape[-2] // 2, shape[-1])
        return self.halve(len(shape) - 3, self.x, [t.reshape(shape) for t in terms])

    def reduce_z(self, groups):
        rows, cols = groups[0][0].shape
        r = rows // self.nz
        n = self.nz
        for bit in range(self.bits):
            at = (self.z // (1 << bit)) % 2
            halves = [
                self.halve(1, at, [t.reshape(n // 2, 2, r, cols) for t in terms])
                for terms in groups
            ]
            send = jnp.stack([h[0] for h in halves])
            n //= 2
            got = self.over_z(send, 1 << bit)
            groups = [h[1] + [got[i]] for i, h in enumerate(halves)]
        return jnp.stack([sum(terms).reshape(r, cols) for terms in groups])

    def all_reduce_z(self, v):
        for bit in range(self.bits):
            v = v + self.over_z(v, 1 << bit)
        return v

    def gather(self, v):
        high = list(range(self.bits))[:0:-1]
        for bit in high[:-1]:
            v = jnp.stack([v, self.over_z(v, 1 << bit)])
        if high:
            got = self.over_z(v, 1 << high[-1])
            two = [jnp.stack([v[..., i, :, :], got[..., i, :, :]]) for i in range(2)]
        else:
            two = [v[..., i, :, :] for i in range(2)]
        two = [t.reshape((-1,) + t.shape[-2:]) for t in two]
        got0 = self.over_x(two[0])
        got1 = self.over_z(two[1], 1)
        two = [jnp.concatenate([two[0], got0]), jnp.concatenate([two[1], got1])]
        got0 = self.over_z(two[0], 1)
        got1 = self.over_x(two[1])
        stacks = [two[0], got0, two[1], got1]
        stacks = stacks + [self.over_core(t) for t in stacks]
        base = self.placed(high, False)
        moves = []
        for dc in range(2):
            group0 = [(0, dc, dx, dz) for dx in range(2) for _, dz in base]
            group1 = [(1, dc, 0, dz ^ low) for low in range(2) for _, dz in base]
            moves += [group0, [(g, c, dx, dz ^ 1) for g, c, dx, dz in group0]]
            moves += [group1, [(g, c, 1 - dx, dz) for g, c, dx, dz in group1]]
        return stacks, moves

    def placed(self, bits, with_x):
        out = []
        names = list(bits) + (["x"] if with_x else [])
        for i in range(1 << len(names)):
            at = [(i >> k) & 1 for k in range(len(names))]
            dz = sum(a << n for a, n in zip(at, names) if n != "x")
            dx = sum(a for a, n in zip(at, names) if n == "x")
            out.append((dx, dz))
        return out

    def join(self, stacks, moves, put, outs, scratch=(), finish=None):
        nz = self.nz
        n_out = len(outs)

        def kernel(pos, *refs):
            ins, refs = refs[: len(stacks)], refs[len(stacks) :]
            for core in range(2):

                @pl.when(pos[0] == core)
                def _():
                    for ref, places in zip(ins, moves):
                        for k, (group, dc, dx, dz) in enumerate(places):
                            row = (pos[1] ^ dx) * nz + (pos[2] ^ dz)
                            put(ref.at[k], group, core ^ dc, row, refs)

            if finish is not None:
                finish(refs)

        return pl.pallas_call(
            kernel,
            out_shape=[jax.ShapeDtypeStruct(s, F32) for s in outs],
            grid_spec=pltpu.PrefetchScalarGridSpec(
                num_scalar_prefetch=1,
                grid=(1,),
                in_specs=[fixed(a.shape) for a in stacks],
                out_specs=[fixed(s) for s in outs],
                scratch_shapes=list(scratch),
            ),
            compiler_params=pltpu.CompilerParams(vmem_limit_bytes=8 * MIB),
        )(ints(self.core, self.x, self.z), *stacks)

    def join_attn(self, stacks, moves, d):
        r = stacks[0].shape[1]
        rows = 2 * self.nz * r

        def put(ref, group, core, row, refs):
            at = pl.ds(pl.multiple_of(row * r, 8), r)
            k = 2 * core + group
            if k < 3:
                refs[0][at, k * d : (k + 1) * d] = ref[...]
            else:
                refs[1][at, :] = ref[...]

        return self.join(stacks, moves, put, [(rows, 3 * d), (rows, d)])

    def join_mlp(self, stacks, moves):
        _, r, cols = stacks[0].shape
        rows = 2 * self.nz * r

        def put(ref, group, core, row, refs):
            at = pl.multiple_of(row * r, 8)
            if group == 0:
                refs[2][pl.ds(core * rows + at, r), :] = ref[...]
            else:
                refs[1][pl.ds(at, r), core * cols : (core + 1) * cols] = ref[...]

        def finish(refs):
            refs[0][...] = refs[2][...].T

        outs = [(cols, 2 * rows), (rows, 2 * cols)]
        scratch = [pltpu.VMEM((2 * rows, cols), F32)]
        return self.join(stacks, moves, put, outs, scratch, finish)


def pick(v, i, axis=0):
    return lax.dynamic_index_in_dim(v, i, axis, keepdims=False)


def whole_mesh_step(n_fsdp, x, vec, b1f, wqkv, wproj, wfc1, wfc2, dy):
    def gather(w):
        return lax.all_gather(w, "fsdp", axis=0, tiled=True)

    def total(v):
        part = lax.psum_scatter(v, "fsdp", scatter_dimension=0, tiled=True)
        return lax.psum(part, "dp")[0]

    zero = ints(0)
    d = x.shape[2]
    w_qkv, w_2 = (zero, [gather(wqkv)]), (zero, [gather(wfc2)])
    joint = zero, [gather(wproj), gather(wfc1)]
    qkv = qkv_call(x, vec, w_qkv)
    ctx, ph, p_lo = attn_fwd(qkv, zero)
    out, mid, dh2, gb1, gb2, send2, keep2, send1, keep1 = mlp(
        x, ctx, dy, vec, b1f, joint, w_2, zero, n_fsdp
    )
    gwp, gva, dmid, dctx = mlp_mid(dh2, ctx, dy, mid, vec, joint)
    dj, *parts = attn_bwd(x, qkv, ph, p_lo, ctx, dctx, vec, gwp, zero, n_fsdp)
    gs, dx = input_grad(x, dj, dmid, vec, w_qkv, gva, gb1, gb2, n_fsdp)
    ga = jnp.concatenate([total(parts[i]) for i in (1, 3, 0, 2)], axis=1)
    gw1 = jnp.concatenate([total(keep1), total(send1)], axis=1)
    gw2 = jnp.concatenate([total(keep2), total(send2)], axis=0).T
    return out, dx, ga[:, : 3 * d], ga[:, 3 * d :], gw1, gw2, small_grads(total(gs))


def pair_step(n_dp, x, vec, b1f, wqkv, wproj, wfc1, wfc2, dy):
    c = Pairs(n_dp)
    core = ints(c.core)
    d = x.shape[2]
    z0 = c.z % 2
    came = c.over_y(c.quarter(wqkv, c.x))
    w_qkv = c.quarter_offs(wqkv.shape[0], c.x), [wqkv, *c.finish(came, c.over_x)]
    joint = [c.quarter(wfc1, c.x), c.quarter(wproj, c.x)]
    joint = c.over_y(jnp.concatenate(joint, axis=1))
    w_2 = c.over_y(c.quarter(wfc2, z0))
    qkv = qkv_call(x, vec, w_qkv)
    pieces = c.finish(tie(joint, qkv), c.over_x)
    joint = c.quarter_offs(wproj.shape[0], c.x), [wproj, wfc1, *pieces]
    ctx, ph, p_lo = attn_fwd(qkv, core)
    pieces = c.finish(tie(w_2, qkv), lambda v: c.over_z(v, 1))
    w_2 = c.quarter_offs(wfc2.shape[0], z0), [wfc2, *pieces]
    out, mid, dh2, gb1, gb2, send2, keep2, send1, keep1 = mlp(
        x, ctx, dy, vec, b1f, joint, w_2, core, 2
    )
    got2 = c.over_core(send2)
    got1 = c.over_core(send1)
    gwp, gva, dmid, dctx = mlp_mid(dh2, ctx, dy, mid, vec, joint)
    send2, keep2 = c.halve_x([got2, keep2])
    send1, keep1 = c.halve_y([got1, keep1])
    got2 = c.over_x(send2)
    got1 = c.over_y(send1)
    dctx = tie(dctx, send1, send2)
    dj, send3, keep3, send4, keep4 = attn_bwd(x, qkv, ph, p_lo, ctx, dctx, vec, gwp, core, 2)
    got3 = c.over_core(send3)
    got4 = c.over_core(send4)
    send2, keep2 = c.halve_y([got2, *keep2])
    send1, keep1 = c.halve_x([got1, *keep1])
    got2 = c.over_y(send2)
    got1 = c.over_x(send1)
    dj = tie(dj, send3, send4, send1, send2)
    gs, dx = input_grad(x, dj, dmid, vec, w_qkv, gva, gb1, gb2, 2)
    send3, keep3 = c.halve_x([got3, keep3])
    send4, keep4 = c.halve_y([got4, keep4])
    got3 = c.over_x(send3)
    got4 = c.over_y(send4)
    gs = gs + c.over_core(tie(gs, send3, send4))
    gs_y = c.over_y(pick(gs, 1 - c.y))
    gs = pick(gs, c.y) + gs_y
    gs_x = c.over_x(gs)
    f = c.reduce_z([[got2, *keep2], [got1, *keep1]])
    f, moves_f = c.gather(f)
    send3, keep3 = c.halve_y([got3, *keep3])
    send4, keep4 = c.halve_x([got4, *keep4])
    got3 = c.over_y(send3)
    got4 = c.over_x(send4)
    a = c.reduce_z([[got3, *keep3], [got4, *keep4]])
    gs = c.all_reduce_z(gs + gs_x)
    a, moves_a = c.gather(a)
    gw2, gw1 = c.join_mlp(f, moves_f)
    gwqkv, gwproj = c.join_attn(a, moves_a, d)
    return out, dx, gwqkv, gwproj, gw1, gw2, small_grads(gs)


def small_grads(gs):
    return [*(gs[i] for i in range(8)), gs[8:].reshape(-1)]


def is_pairs(n_dp, n_fsdp):
    return n_fsdp == 2 and n_dp >= 8 and (n_dp & (n_dp - 1)) == 0


def body(n_dp, n_fsdp, x, g1, s1, wqkv, qb, vb, wproj, pb, g2, s2, wfc1, b1, wfc2, b2, dy):
    pairs = is_pairs(n_dp, n_fsdp)
    w = g1.shape[0]
    small = jnp.concatenate([jnp.stack([g1, s1, qb, vb, pb, g2, s2, b2]), b1.reshape(-1, w)])
    if pairs:
        other = swap_with(small, n_dp, n_fsdp, 0, 1)
        is_first = lax.axis_index("fsdp") == 0
        small = jnp.stack([jnp.where(is_first, small, other), jnp.where(is_first, other, small)])
    else:
        small = lax.all_gather(small, "fsdp", axis=0)
    vec = small[:, :8].transpose(1, 0, 2).reshape(8, -1)
    b1f = small[:, 8:].reshape(1, -1)
    args = (x, vec, b1f, wqkv, wproj, wfc1, wfc2, dy)
    step = pair_step(n_dp, *args) if pairs else whole_mesh_step(n_fsdp, *args)
    out, dx, gwqkv, gwproj, gw1, gw2, gs = step
    return (
        out,
        dx,
        gs[0],
        gs[1],
        gwqkv,
        gs[2],
        gs[3],
        gwproj,
        gs[4],
        gs[5],
        gs[6],
        gw1,
        gs[8],
        gw2,
        gs[7],
    )


def solution(mesh):
    n_dp, n_fsdp = mesh.shape["dp"], mesh.shape["fsdp"]
    act = P(("dp", "fsdp"), None, None)
    vec = P("fsdp")
    mat = P("fsdp", None)
    in_specs = (act, vec, vec, mat, vec, vec, mat, vec, vec, vec, mat, vec, mat, vec, act)
    out_specs = (act,) + in_specs[:1] + in_specs[1:14]
    return jax.shard_map(
        lambda *a: body(n_dp, n_fsdp, *a),
        mesh=mesh,
        in_specs=in_specs,
        out_specs=out_specs,
        check_vma=False,
    )
```

```python
import math

import jax
import jax.numpy as jnp
from jax import lax
from jax.experimental import pallas as pl
from jax.experimental.pallas import tpu as pltpu
from jax.sharding import PartitionSpec as P


HEAD_DIM = 64
LANES = 128
EPS = 1e-06
F32 = jnp.float32
BF16 = jnp.bfloat16
MIB = 1 << 20


def split(v):
    hi = v.astype(BF16)
    lo = (v - hi.astype(F32)).astype(BF16)
    return hi, lo


def dot(a, b, ca, cb):
    return lax.dot_general(a, b, (((ca,), (cb,)), ((), ())), preferred_element_type=F32)


def dot3(a, b, ca, cb):
    ah, al = a
    bh, bl = b
    return dot(ah, bh, ca, cb) + (dot(ah, bl, ca, cb) + dot(al, bh, ca, cb))


def row_sum(v):
    return jnp.sum(v, axis=0, keepdims=True)


def norm_parts(v):
    center = v - jnp.mean(v, axis=-1, keepdims=True)
    inv = lax.rsqrt(jnp.mean(center * center, axis=-1, keepdims=True) + EPS)
    return center * inv, inv


def norm_back(dh, n, inv, gain):
    s = dh * gain
    return inv * (
        s - jnp.mean(s, axis=-1, keepdims=True) - n * jnp.mean(s * n, axis=-1, keepdims=True)
    )


def load_weight(offs, k, pieces, hi_ref, lo_ref):
    for p in pieces:
        at = pl.multiple_of(offs[k], 16)
        hi, lo = split(p[...])
        hi_ref[pl.ds(at, p.shape[0]), :] = hi
        lo_ref[pl.ds(at, p.shape[0]), :] = lo
        k += 1
    return k


def load_rows(offs, k, pieces, ref):
    n = ref.shape[0] // 3
    for p in pieces:
        hi, lo = split(p[...])
        for base, part in ((0, hi), (n, hi), (2 * n, lo)):
            ref[pl.ds(pl.multiple_of(base + offs[k], 16), p.shape[0]), :] = part
        k += 1


def load_cols(offs, k, pieces, ref):
    n = ref.shape[1] // 3
    for p in pieces:
        at = pl.ds(pl.multiple_of(offs[k], 16), p.shape[0])
        hi, lo = split(p[...])
        ref[at, :n] = hi
        ref[at, n : 2 * n] = hi
        ref[at, 2 * n :] = lo
        k += 1


def tall(v):
    hi, lo = split(v)
    return jnp.concatenate([hi, lo, hi], axis=1)


def fold(t):
    n = t.shape[1] // 2
    return t[:, :n] + t[:, n:]


def dot_rows(v, w3):
    hi, lo = split(v)
    n = w3.shape[0] // 3
    return fold(dot(hi, w3[n:], 1, 1)) + dot(lo, w3[:n], 1, 1)


def dot_outer(v3, w):
    n = v3.shape[1] // 3
    t = dot(v3[:, : 2 * n], w[0], 0, 0)
    return t[:n] + (t[n:] + dot(v3[:, :n], w[1], 0, 0))


def both(hi_ref, lo_ref):
    return hi_ref[...], lo_ref[...]


def lane_lt(shape):
    return lax.broadcasted_iota(jnp.int32, shape, 1) < HEAD_DIM


def swap(v):
    return pltpu.roll(v, HEAD_DIM, 1)


def pair_left(v, low):
    hi = v.astype(BF16).astype(F32)
    lo = v - hi
    zero = jnp.zeros_like(v)
    h0 = jnp.concatenate([jnp.where(low, hi, swap(lo)), jnp.where(low, hi, zero)], axis=1)
    h1 = jnp.concatenate([jnp.where(low, swap(lo), hi), jnp.where(low, zero, hi)], axis=1)
    return h0.astype(BF16), h1.astype(BF16)


def pair_right(v, low):
    hi = v.astype(BF16).astype(F32)
    lo = v - hi
    rolled = swap(hi)
    h0 = jnp.concatenate([jnp.where(low, hi, rolled), lo], axis=1)
    h1 = jnp.concatenate([jnp.where(low, rolled, hi), lo], axis=1)
    return h0.astype(BF16), h1.astype(BF16)


def wide(v):
    hi, lo = split(v)
    return hi, jnp.concatenate([hi, lo], axis=1)


def dot_wide(ph, pl_, w, ca):
    hi, cat = w
    t = dot(ph, cat, ca, 0)
    return t[:, :LANES] + (t[:, LANES:] + dot(pl_, hi, ca, 0))


def part_rows(g_ref, send_ref, keep_ref, core):
    n, rows, cols = keep_ref.shape
    for i in range(n):
        lanes = slice(i * cols, (i + 1) * cols)
        send_ref[i] = g_ref[pl.ds(pl.multiple_of((1 - core) * rows, 8), rows), lanes]
        keep_ref[i] = g_ref[pl.ds(pl.multiple_of(core * rows, 8), rows), lanes]


def part_cols(g_ref, send_ref, keep_ref, core, group=0):
    n, rows, cols = keep_ref.shape
    half = g_ref.shape[1] // 2
    for i in range(n):
        at = pl.multiple_of((1 - core) * half + group * cols, LANES)
        send_ref[i] = g_ref[i * rows : (i + 1) * rows, pl.ds(at, cols)]
        at = pl.multiple_of(core * half + group * cols, LANES)
        keep_ref[i] = g_ref[i * rows : (i + 1) * rows, pl.ds(at, cols)]


def last():
    return pl.program_id(0) == pl.num_programs(0) - 1


def first():
    return pl.program_id(0) == 0


def qkv_kernel(np_, offs, x_ref, vec_ref, *refs):
    w_pieces = refs[:np_]
    qkv_ref, w3 = refs[np_:]

    @pl.when(first())
    def _():
        load_rows(offs, 0, w_pieces, w3)

    d = x_ref.shape[2]
    vec = vec_ref[...]
    n1, _ = norm_parts(x_ref[0])
    h1 = n1 * vec[0:1] + vec[1:2]
    qkv = dot(tall(h1), w3[...], 1, 0)
    qkv_ref[0, :, :d] = qkv[:, :d] + vec[2:3]
    qkv_ref[0, :, d : 2 * d] = qkv[:, d : 2 * d]
    qkv_ref[0, :, 2 * d :] = qkv[:, 2 * d :] + vec[3:4]


def attn_fwd_kernel(offs, qkv_ref, ctx_ref, ph_ref, pl_ref):
    d = ctx_ref.shape[2]
    low = lane_lt((qkv_ref.shape[1], LANES))
    for j in range(d // LANES):
        sl = slice(j * LANES, (j + 1) * LANES)
        q = qkv_ref[0, :, sl] * (1.0 / math.sqrt(HEAD_DIM))
        k = qkv_ref[0, :, d + j * LANES : d + (j + 1) * LANES]
        v = qkv_ref[0, :, 2 * d + j * LANES : 2 * d + (j + 1) * LANES]
        qs = pair_left(q, low)
        ks = pair_right(k, low)
        vw = wide(v)
        outs = []
        for i in range(2):
            s = dot(qs[i], ks[i], 1, 1)
            e = jnp.exp(s - jnp.max(s, axis=-1, keepdims=True))
            p = e * (1.0 / jnp.sum(e, axis=-1, keepdims=True))
            hi, lo = split(p)
            ph_ref[0, 2 * j + i] = hi
            pl_ref[0, 2 * j + i] = lo
            outs.append(dot_wide(hi, lo, vw, 1))
        ctx_ref[0, :, sl] = jnp.where(low, outs[0], outs[1])


def fill_rows(buf_ref, ref):
    n, s, _ = ref.shape
    step = buf_ref.shape[0] // n
    buf_ref[...] = jnp.zeros_like(buf_ref)
    for i in range(n):
        buf_ref[i * step : i * step + s, :] = ref[i]


def take_rows(ref, rows_ref):
    n, s, _ = ref.shape
    step = rows_ref.shape[0] // n
    for i in range(n):
        ref[i] = rows_ref[i * step : i * step + s, :]


def mlp_kernel(np_, offs, x_ref, ctx_ref, dy_ref, vec_ref, b1_ref, wp, w1, *refs):
    n, n2 = np_
    pp, p1, p2 = refs[:n], refs[n : 2 * n], refs[2 * n : 2 * n + n2]
    refs = refs[2 * n + n2 :]
    out_ref, mid_ref, dh2_ref, gb1_ref, gb2_ref = refs[:5]
    send2_ref, keep2_ref, send1_ref, keep1_ref = refs[5:9]
    wph, wpl, w1r, w2c, h3, y3, mids, outs, dh2s, g2_ref, g1_ref = refs[9:]
    i = pl.program_id(0)
    d = x_ref.shape[2]
    cols = b1_ref.shape[1]
    at = pl.ds(pl.multiple_of(i * cols, LANES), cols)

    @pl.when(first())
    def _():
        vec = vec_ref[...]
        load_weight(offs, 0, [wp, *pp], wph, wpl)
        load_cols(offs, n + 1, p2, w2c)
        fill_rows(outs, ctx_ref)
        fill_rows(mids, x_ref)
        mid = mids[...] + dot3(split(outs[...]), both(wph, wpl), 1, 0) + vec[4:5]
        mids[...] = mid
        n2, _ = norm_parts(mid)
        h3[...] = tall(n2 * vec[5:6] + vec[6:7])
        fill_rows(dh2s, dy_ref)
        dy = dh2s[...]
        y3[...] = tall(dy)
        gb2_ref[...] = row_sum(dy)
        outs[...] = mid + vec[7:8]
        dh2s[...] = jnp.zeros_like(dh2s)

    load_rows(offs, 0, [w1, *p1], w1r)
    pre = dot(h3[...], w1r[...], 1, 0) + b1_ref[...]
    half = 0.5 * (1.0 + lax.erf(pre * (1.0 / math.sqrt(2.0))))
    act = split(pre * half)
    slope = half + pre * jnp.exp(-0.5 * pre * pre) * (1.0 / math.sqrt(2.0 * math.pi))
    outs[...] += fold(dot(act[0], w2c[at, d:], 1, 0)) + dot(act[1], w2c[at, :d], 1, 0)
    g2_ref[:, at] = dot_outer(y3[...], act)
    dpre = dot(y3[...], w2c[at, :], 1, 1) * slope
    gb1_ref[...] = row_sum(dpre)
    dh2s[...] += dot_rows(dpre, w1r[...])
    g1_ref[:, at] = dot_outer(h3[...], split(dpre))

    @pl.when(last())
    def _():
        take_rows(out_ref, outs)
        take_rows(mid_ref, mids)
        take_rows(dh2_ref, dh2s)
        core = offs[n + 1 + len(p2)]
        part_rows(g2_ref, send2_ref, keep2_ref, core)
        part_cols(g1_ref, send1_ref, keep1_ref, core)


def mid_kernel(np_, offs, dh2_ref, ctx_ref, dy_ref, mid_ref, vec_ref, *refs):
    gp_ref, gv_ref, dmid_ref, dctx_ref, wph, wpl = refs[np_:]

    @pl.when(first())
    def _():
        load_weight(offs, 0, refs[:np_], wph, wpl)
        gp_ref[...] = jnp.zeros_like(gp_ref)
        gv_ref[...] = jnp.zeros_like(gv_ref)

    n2, inv2 = norm_parts(mid_ref[0])
    dh2 = dh2_ref[0]
    dmid = dy_ref[0] + norm_back(dh2, n2, inv2, vec_ref[5:6])
    dmid_ref[0] = dmid
    gv_ref[0:1] += row_sum(dmid)
    gv_ref[1:2] += row_sum(dh2 * n2)
    gv_ref[2:3] += row_sum(dh2)
    dmid = split(dmid)
    gp_ref[...] += dot3(split(ctx_ref[0]), dmid, 0, 0)
    dctx_ref[0] = dot3(dmid, both(wph, wpl), 1, 1)


def attn_bwd_kernel(
    offs, x_ref, qkv_ref, ph_ref, pl_ref, ctx_ref, dctx_ref, vec_ref, gp_ref, *refs
):
    dj_ref, send0_ref, keep0_ref, send1_ref, keep1_ref, g_ref = refs
    d = ctx_ref.shape[2]

    @pl.when(first())
    def _():
        g_ref[:, : 3 * d] = jnp.zeros((d, 3 * d), F32)
        g_ref[:, 3 * d :] = gp_ref[...]

    scale = 1.0 / math.sqrt(HEAD_DIM)
    low = lane_lt((ctx_ref.shape[1], LANES))
    for j in range(d // LANES):
        sl = slice(j * LANES, (j + 1) * LANES)
        q = qkv_ref[0, :, j * LANES : (j + 1) * LANES] * scale
        k = qkv_ref[0, :, d + j * LANES : d + (j + 1) * LANES]
        v = qkv_ref[0, :, 2 * d + j * LANES : 2 * d + (j + 1) * LANES]
        dc = dctx_ref[0, :, sl]
        prod = dc * ctx_ref[0, :, sl]
        delta0 = jnp.sum(jnp.where(low, prod, 0.0), axis=-1, keepdims=True)
        delta1 = jnp.sum(jnp.where(low, 0.0, prod), axis=-1, keepdims=True)
        deltas = (delta0, delta1)
        dcs = pair_left(dc, low)
        vs = pair_right(v, low)
        qw, kw, dcw = wide(q), wide(k), wide(dc)
        dq, dk, dv = [], [], []
        for i in range(2):
            ph = ph_ref[0, 2 * j + i]
            p_lo = pl_ref[0, 2 * j + i]
            dp = dot(dcs[i], vs[i], 1, 1)
            ds = (ph.astype(F32) + p_lo.astype(F32)) * (dp - deltas[i])
            dsh, dsl = split(ds)
            dv.append(dot_wide(ph, p_lo, dcw, 0))
            dq.append(dot_wide(dsh, dsl, kw, 1))
            dk.append(dot_wide(dsh, dsl, qw, 0))
        dj_ref[0, :, sl] = jnp.where(low, dq[0], dq[1]) * scale
        dj_ref[0, :, d + j * LANES : d + (j + 1) * LANES] = jnp.where(low, dk[0], dk[1])
        dj_ref[0, :, 2 * d + j * LANES : 2 * d + (j + 1) * LANES] = jnp.where(low, dv[0], dv[1])
    n1, _ = norm_parts(x_ref[0])
    h1 = n1 * vec_ref[0:1] + vec_ref[1:2]
    g_ref[:, : 3 * d] += dot_outer(tall(h1), split(dj_ref[0]))

    @pl.when(last())
    def _():
        part_cols(g_ref, send0_ref, keep0_ref, offs[0], 0)
        part_cols(g_ref, send1_ref, keep1_ref, offs[0], 1)


def input_grad_kernel(np_, offs, x_ref, dj_ref, dmid_ref, vec_ref, *refs):
    w_pieces = refs[:np_]
    gva_ref, gb1_ref, gb2_ref = refs[np_ : np_ + 3]
    gs_ref, dx_ref, w3, gv_ref = refs[np_ + 3 :]

    @pl.when(first())
    def _():
        load_rows(offs, 0, w_pieces, w3)
        gv_ref[...] = jnp.zeros_like(gv_ref)

    d = x_ref.shape[2]
    n1, inv1 = norm_parts(x_ref[0])
    dj = dj_ref[0]
    sums = row_sum(dj)
    gv_ref[2:3] += sums[:, :d]
    gv_ref[3:4] += sums[:, 2 * d :]
    dh1 = dot_rows(dj, w3[...])
    gv_ref[0:1] += row_sum(dh1 * n1)
    gv_ref[1:2] += row_sum(dh1)
    dx_ref[0] = dmid_ref[0] + norm_back(dh1, n1, inv1, vec_ref[0:1])

    @pl.when(last())
    def _():
        shards, _, w = gs_ref.shape
        per = gb1_ref.shape[1] // (shards * w)
        for h in range(shards):
            sl = slice(h * w, (h + 1) * w)
            gs_ref[h, 0:4] = gv_ref[0:4, sl]
            gs_ref[h, 4:7] = gva_ref[0:3, sl]
            gs_ref[h, 7:8] = gb2_ref[:, sl]
            for j in range(per):
                at = (h * per + j) * w
                gs_ref[h, 8 + j : 9 + j] = gb1_ref[:, at : at + w]


def per_image(shape):
    n = len(shape)
    return pl.BlockSpec((1,) + tuple(shape[1:]), lambda i, offs: (i,) + (0,) * (n - 1))


def fixed(shape):
    n = len(shape)
    return pl.BlockSpec(tuple(shape), lambda i, offs: (0,) * n)


def block_at(shape, col):
    return pl.BlockSpec(shape, lambda i, offs: (0, col))


def run(kernel, offs, images, consts, outs, scratch, flops, blocks={}, vmem=12):
    count = images[0].shape[0]
    in_specs = [per_image(a.shape) for a in images] + [
        block_at(*blocks[i]) if i in blocks else fixed(a.shape) for i, a in enumerate(consts)
    ]
    out_specs = [per_image(s) if im else fixed(s) for s, _, im in outs]
    return pl.pallas_call(
        kernel,
        out_shape=[jax.ShapeDtypeStruct(s, t) for s, t, _ in outs],
        grid_spec=pltpu.PrefetchScalarGridSpec(
            num_scalar_prefetch=1,
            grid=(count,),
            in_specs=in_specs,
            out_specs=out_specs,
            scratch_shapes=scratch,
        ),
        cost_estimate=pl.CostEstimate(flops=flops, transcendentals=0, bytes_accessed=8 << 20),
        compiler_params=pltpu.CompilerParams(
            dimension_semantics=("arbitrary",), vmem_limit_bytes=vmem * MIB
        ),
    )(offs, *images, *consts)


def pair_scratch(rows, cols):
    return [pltpu.VMEM((rows, cols), BF16), pltpu.VMEM((rows, cols), BF16)]


def image(*shape, dtype=F32):
    return (shape, dtype, True)


def const(*shape):
    return (shape, F32, False)


def qkv_call(x, vec, w):
    offs, pieces = w
    b, s, d = x.shape
    return run(
        lambda *r: qkv_kernel(len(pieces), *r),
        offs,
        [x],
        [vec, *pieces],
        [image(b, s, 3 * d)],
        [pltpu.VMEM((3 * d, 3 * d), BF16)],
        18 * b * s * d * d,
    )[0]


def attn_fwd(qkv, zero):
    b, s, d = qkv.shape
    d = d // 3
    heads = d // HEAD_DIM
    probs = image(b, heads, s, s, dtype=BF16)
    return run(
        attn_fwd_kernel, zero, [qkv], [], [image(b, s, d), probs, probs], [],
        30 * b * s * d * d, vmem=56,
    )


def cols_block(shape, cols, at):
    return pl.BlockSpec((shape[0], cols), lambda i, offs: (0, at(i)))


def mlp(x, ctx, dy, vec, b1, joint, w2, core, shards):
    offs, (wp, w1, *pieces) = joint
    b, s, d = x.shape
    ff = b1.shape[1]
    rows = b * (-(-s // 8) * 8)
    c = ff // 3
    half2, half1 = (shards, d // 2, ff // shards), (shards, d // shards, ff // 2)
    shapes = [(b, s, d), (b, s, d), (b, s, d), (1, ff), (1, d), half2, half2, half1, half1]
    n = len(pieces)
    specs = [fixed(a.shape) for a in (x, ctx, dy, vec)]
    specs += [cols_block(b1.shape, c, lambda i: i), fixed(wp.shape)]
    specs += [cols_block(w1.shape, c, lambda i: i)]
    specs += [cols_block(p.shape, d, lambda i: ff // d) for p in pieces]
    specs += [cols_block(p.shape, c, lambda i: i) for p in pieces]
    specs += [fixed(p.shape) for p in w2[1]]
    out_specs = [fixed(t) for t in shapes]
    out_specs[3] = cols_block((1, ff), c, lambda i: i)
    big = pltpu.VMEM((rows, d), F32)
    tall_one = pltpu.VMEM((rows, 3 * d), BF16)
    return pl.pallas_call(
        lambda *r: mlp_kernel((n, len(w2[1])), *r),
        name="mlp",
        out_shape=[jax.ShapeDtypeStruct(t, F32) for t in shapes],
        grid_spec=pltpu.PrefetchScalarGridSpec(
            num_scalar_prefetch=1,
            grid=(ff // c,),
            in_specs=specs,
            out_specs=out_specs,
            scratch_shapes=pair_scratch(d, d)
            + [pltpu.VMEM((3 * d, c), BF16), pltpu.VMEM((ff, 3 * d), BF16)]
            + [tall_one, tall_one, big, big, big]
            + [pltpu.VMEM((d, ff), F32)] * 2,
        ),
        cost_estimate=pl.CostEstimate(
            flops=40 * b * s * d * ff, transcendentals=0, bytes_accessed=8 << 20
        ),
        compiler_params=pltpu.CompilerParams(
            dimension_semantics=("arbitrary",), vmem_limit_bytes=56 * MIB
        ),
    )(
        jnp.concatenate([offs, w2[0], core]),
        *(x, ctx, dy, vec, b1, wp, w1),
        *pieces,
        *pieces,
        *w2[1],
    )


def mlp_mid(dh2, ctx, dy, mid, vec, joint):
    offs, (wp, _, *pieces) = joint
    b, s, d = mid.shape
    return run(
        lambda *r: mid_kernel(1 + len(pieces), *r),
        offs,
        in_hbm([dh2, ctx, dy, mid]),
        [vec, *in_hbm([wp, *pieces])],
        [const(d, d), const(8, d), image(b, s, d), image(b, s, d)],
        pair_scratch(d, d),
        12 * b * s * d * d,
        {2 + i: ((p.shape[0], d), p.shape[1] // d - 1) for i, p in enumerate(pieces)},
    )


def attn_bwd(x, qkv, ph, p_lo, ctx, dctx, vec, gwp, core, shards):
    b, s, d = ctx.shape
    part = const(shards, d // shards, d)
    return run(
        attn_bwd_kernel,
        core,
        [x, qkv, ph, p_lo, ctx, dctx],
        [vec, gwp],
        [image(b, s, 3 * d), part, part, part, part],
        [pltpu.VMEM((d, 4 * d), F32)],
        60 * b * s * d * d,
        vmem=40,
    )


def input_grad(x, dj, dmid, vec, w, gva, gb1, gb2, shards):
    offs, pieces = w
    b, s, d = x.shape
    rows = 8 + gb1.shape[1] // d
    return run(
        lambda *r: input_grad_kernel(len(pieces), *r),
        offs,
        [x, dj, dmid],
        [vec, *pieces, gva, gb1, gb2],
        [const(shards, rows, d // shards), image(b, s, d)],
        [pltpu.VMEM((3 * d, 3 * d), BF16), pltpu.VMEM((8, d), F32)],
        18 * b * s * d * d,
    )


def in_hbm(values):
    return [pltpu.with_memory_space_constraint(v, pltpu.HBM) for v in values]


def tie(v, *after):
    return lax.optimization_barrier((v, *after))[0]


def ints(*values):
    return jnp.stack([jnp.asarray(v, jnp.int32) for v in values])


def swap_with(v, n_dp, n_fsdp, dp_bits, fsdp_bits):
    perm = []
    for i in range(n_dp * n_fsdp):
        d, f = divmod(i, n_fsdp)
        perm.append((i, (d ^ dp_bits) * n_fsdp + (f ^ fsdp_bits)))
    return lax.ppermute(v, ("dp", "fsdp"), perm)


class Pairs:
    def __init__(self, n_dp):
        self.n_dp, self.nz = n_dp, n_dp // 4
        self.bits = self.nz.bit_length() - 1
        dp = lax.axis_index("dp")
        self.core, self.x, self.z = dp % 2, (dp // 2) % 2, dp // 4
        self.y = lax.axis_index("fsdp")

    def over_core(self, v):
        return swap_with(v, self.n_dp, 2, 1, 0)

    def over_x(self, v):
        return swap_with(v, self.n_dp, 2, 2, 0)

    def over_y(self, v):
        return swap_with(v, self.n_dp, 2, 0, 1)

    def over_z(self, v, k):
        return swap_with(v, self.n_dp, 2, 4 * k, 0)

    def quarter(self, w, side):
        rows = w.shape[0] // 4
        return lax.dynamic_slice_in_dim(w, (2 * self.core + side) * rows, rows, 0)

    def quarter_offs(self, rows, side):
        base = (1 - self.y) * rows
        q = rows // 4
        order = [(c, i) for c in (self.core, 1 - self.core) for i in (side, 1 - side)]
        return ints(self.y * rows, *(base + (2 * c + i) * q for c, i in order))

    def finish(self, a, over):
        b = over(a)
        return [a, b, self.over_core(a), self.over_core(b)]

    def halve(self, axis, at, terms):
        return sum(pick(t, 1 - at, axis) for t in terms), [pick(t, at, axis) for t in terms]

    def halve_y(self, terms):
        return self.halve(0, self.y, terms)

    def halve_x(self, terms):
        shape = terms[0].shape
        shape = shape[:-2] + (2, shape[-2] // 2, shape[-1])
        return self.halve(len(shape) - 3, self.x, [t.reshape(shape) for t in terms])

    def reduce_z(self, groups):
        rows, cols = groups[0][0].shape
        r = rows // self.nz
        n = self.nz
        for bit in range(self.bits):
            at = (self.z // (1 << bit)) % 2
            halves = [
                self.halve(1, at, [t.reshape(n // 2, 2, r, cols) for t in terms])
                for terms in groups
            ]
            send = jnp.stack([h[0] for h in halves])
            n //= 2
            got = self.over_z(send, 1 << bit)
            groups = [h[1] + [got[i]] for i, h in enumerate(halves)]
        return jnp.stack([sum(terms).reshape(r, cols) for terms in groups])

    def all_reduce_z(self, v):
        for bit in range(self.bits):
            v = v + self.over_z(v, 1 << bit)
        return v

    def gather(self, v):
        high = list(range(self.bits))[:0:-1]
        for bit in high[:-1]:
            v = jnp.stack([v, self.over_z(v, 1 << bit)])
        if high:
            got = self.over_z(v, 1 << high[-1])
            two = [jnp.stack([v[..., i, :, :], got[..., i, :, :]]) for i in range(2)]
        else:
            two = [v[..., i, :, :] for i in range(2)]
        two = [t.reshape((-1,) + t.shape[-2:]) for t in two]
        got0 = self.over_x(two[0])
        got1 = self.over_z(two[1], 1)
        two = [jnp.concatenate([two[0], got0]), jnp.concatenate([two[1], got1])]
        got0 = self.over_z(two[0], 1)
        got1 = self.over_x(two[1])
        stacks = [two[0], got0, two[1], got1]
        stacks = stacks + [self.over_core(t) for t in stacks]
        base = self.placed(high, False)
        moves = []
        for dc in range(2):
            group0 = [(0, dc, dx, dz) for dx in range(2) for _, dz in base]
            group1 = [(1, dc, 0, dz ^ low) for low in range(2) for _, dz in base]
            moves += [group0, [(g, c, dx, dz ^ 1) for g, c, dx, dz in group0]]
            moves += [group1, [(g, c, 1 - dx, dz) for g, c, dx, dz in group1]]
        return stacks, moves

    def placed(self, bits, with_x):
        out = []
        names = list(bits) + (["x"] if with_x else [])
        for i in range(1 << len(names)):
            at = [(i >> k) & 1 for k in range(len(names))]
            dz = sum(a << n for a, n in zip(at, names) if n != "x")
            dx = sum(a for a, n in zip(at, names) if n == "x")
            out.append((dx, dz))
        return out

    def join(self, stacks, moves, put, outs, scratch=(), finish=None):
        nz = self.nz
        n_out = len(outs)

        def kernel(pos, *refs):
            ins, refs = refs[: len(stacks)], refs[len(stacks) :]
            for core in range(2):

                @pl.when(pos[0] == core)
                def _():
                    for ref, places in zip(ins, moves):
                        for k, (group, dc, dx, dz) in enumerate(places):
                            row = (pos[1] ^ dx) * nz + (pos[2] ^ dz)
                            put(ref.at[k], group, core ^ dc, row, refs)

            if finish is not None:
                finish(refs)

        return pl.pallas_call(
            kernel,
            out_shape=[jax.ShapeDtypeStruct(s, F32) for s in outs],
            grid_spec=pltpu.PrefetchScalarGridSpec(
                num_scalar_prefetch=1,
                grid=(1,),
                in_specs=[fixed(a.shape) for a in stacks],
                out_specs=[fixed(s) for s in outs],
                scratch_shapes=list(scratch),
            ),
            compiler_params=pltpu.CompilerParams(vmem_limit_bytes=8 * MIB),
        )(ints(self.core, self.x, self.z), *stacks)

    def join_attn(self, stacks, moves, d):
        r = stacks[0].shape[1]
        rows = 2 * self.nz * r

        def put(ref, group, core, row, refs):
            at = pl.ds(pl.multiple_of(row * r, 8), r)
            k = 2 * core + group
            if k < 3:
                refs[0][at, k * d : (k + 1) * d] = ref[...]
            else:
                refs[1][at, :] = ref[...]

        return self.join(stacks, moves, put, [(rows, 3 * d), (rows, d)])

    def join_mlp(self, stacks, moves):
        _, r, cols = stacks[0].shape
        rows = 2 * self.nz * r

        def put(ref, group, core, row, refs):
            at = pl.multiple_of(row * r, 8)
            if group == 0:
                refs[2][pl.ds(core * rows + at, r), :] = ref[...]
            else:
                refs[1][pl.ds(at, r), core * cols : (core + 1) * cols] = ref[...]

        def finish(refs):
            refs[0][...] = refs[2][...].T

        outs = [(cols, 2 * rows), (rows, 2 * cols)]
        scratch = [pltpu.VMEM((2 * rows, cols), F32)]
        return self.join(stacks, moves, put, outs, scratch, finish)


def pick(v, i, axis=0):
    return lax.dynamic_index_in_dim(v, i, axis, keepdims=False)


def whole_mesh_step(n_fsdp, x, vec, b1f, wqkv, wproj, wfc1, wfc2, dy):
    def gather(w):
        return lax.all_gather(w, "fsdp", axis=0, tiled=True)

    def total(v):
        part = lax.psum_scatter(v, "fsdp", scatter_dimension=0, tiled=True)
        return lax.psum(part, "dp")[0]

    zero = ints(0)
    d = x.shape[2]
    w_qkv, w_2 = (zero, [gather(wqkv)]), (zero, [gather(wfc2)])
    joint = zero, [gather(wproj), gather(wfc1)]
    qkv = qkv_call(x, vec, w_qkv)
    ctx, ph, p_lo = attn_fwd(qkv, zero)
    out, mid, dh2, gb1, gb2, send2, keep2, send1, keep1 = mlp(
        x, ctx, dy, vec, b1f, joint, w_2, zero, n_fsdp
    )
    gwp, gva, dmid, dctx = mlp_mid(dh2, ctx, dy, mid, vec, joint)
    dj, *parts = attn_bwd(x, qkv, ph, p_lo, ctx, dctx, vec, gwp, zero, n_fsdp)
    gs, dx = input_grad(x, dj, dmid, vec, w_qkv, gva, gb1, gb2, n_fsdp)
    ga = jnp.concatenate([total(parts[i]) for i in (1, 3, 0, 2)], axis=1)
    gw1 = jnp.concatenate([total(keep1), total(send1)], axis=1)
    gw2 = jnp.concatenate([total(keep2), total(send2)], axis=0).T
    return out, dx, ga[:, : 3 * d], ga[:, 3 * d :], gw1, gw2, small_grads(total(gs))


def pair_step(n_dp, x, vec, b1f, wqkv, wproj, wfc1, wfc2, dy):
    c = Pairs(n_dp)
    core = ints(c.core)
    d = x.shape[2]
    z0 = c.z % 2
    came = c.over_y(c.quarter(wqkv, c.x))
    w_qkv = c.quarter_offs(wqkv.shape[0], c.x), [wqkv, *c.finish(came, c.over_x)]
    joint = [c.quarter(wfc1, c.x), c.quarter(wproj, c.x)]
    joint = c.over_y(jnp.concatenate(joint, axis=1))
    w_2 = c.over_y(c.quarter(wfc2, z0))
    qkv = in_hbm([qkv_call(x, vec, w_qkv)])[0]
    pieces = c.finish(tie(joint, qkv), c.over_x)
    joint = c.quarter_offs(wproj.shape[0], c.x), [wproj, wfc1, *pieces]
    ctx, ph, p_lo = attn_fwd(qkv, core)
    pieces = c.finish(tie(w_2, qkv), lambda v: c.over_z(v, 1))
    w_2 = c.quarter_offs(wfc2.shape[0], z0), [wfc2, *pieces]
    out, mid, dh2, gb1, gb2, send2, keep2, send1, keep1 = mlp(
        x, ctx, dy, vec, b1f, joint, w_2, core, 2
    )
    got2 = c.over_core(send2)
    got1 = c.over_core(send1)
    gwp, gva, dmid, dctx = mlp_mid(dh2, ctx, dy, mid, vec, joint)
    send2, keep2 = c.halve_x([got2, keep2])
    send1, keep1 = c.halve_y([got1, keep1])
    got2 = c.over_x(send2)
    got1 = c.over_y(send1)
    dctx = tie(dctx, send1, send2)
    dj, send3, keep3, send4, keep4 = attn_bwd(x, qkv, ph, p_lo, ctx, dctx, vec, gwp, core, 2)
    got3 = c.over_core(send3)
    got4 = c.over_core(send4)
    send2, keep2 = c.halve_y([got2, *keep2])
    send1, keep1 = c.halve_x([got1, *keep1])
    got2 = c.over_y(send2)
    got1 = c.over_x(send1)
    dj = tie(dj, send3, send4, send1, send2)
    gs, dx = input_grad(x, dj, dmid, vec, w_qkv, gva, gb1, gb2, 2)
    send3, keep3 = c.halve_x([got3, keep3])
    send4, keep4 = c.halve_y([got4, keep4])
    got3 = c.over_x(send3)
    got4 = c.over_y(send4)
    gs = gs + c.over_core(tie(gs, send3, send4))
    gs_y = c.over_y(pick(gs, 1 - c.y))
    gs = pick(gs, c.y) + gs_y
    gs_x = c.over_x(gs)
    f = c.reduce_z([[got2, *keep2], [got1, *keep1]])
    f, moves_f = c.gather(f)
    send3, keep3 = c.halve_y([got3, *keep3])
    send4, keep4 = c.halve_x([got4, *keep4])
    got3 = c.over_y(send3)
    got4 = c.over_x(send4)
    a = c.reduce_z([[got3, *keep3], [got4, *keep4]])
    gs = c.all_reduce_z(gs + gs_x)
    a, moves_a = c.gather(a)
    gw2, gw1 = c.join_mlp(f, moves_f)
    gwqkv, gwproj = c.join_attn(a, moves_a, d)
    return out, dx, gwqkv, gwproj, gw1, gw2, small_grads(gs)


def small_grads(gs):
    return [*(gs[i] for i in range(8)), gs[8:].reshape(-1)]


def is_pairs(n_dp, n_fsdp):
    return n_fsdp == 2 and n_dp >= 8 and (n_dp & (n_dp - 1)) == 0


def body(n_dp, n_fsdp, x, g1, s1, wqkv, qb, vb, wproj, pb, g2, s2, wfc1, b1, wfc2, b2, dy):
    pairs = is_pairs(n_dp, n_fsdp)
    w = g1.shape[0]
    small = jnp.concatenate([jnp.stack([g1, s1, qb, vb, pb, g2, s2, b2]), b1.reshape(-1, w)])
    if pairs:
        other = swap_with(small, n_dp, n_fsdp, 0, 1)
        is_first = lax.axis_index("fsdp") == 0
        small = jnp.stack([jnp.where(is_first, small, other), jnp.where(is_first, other, small)])
    else:
        small = lax.all_gather(small, "fsdp", axis=0)
    vec = small[:, :8].transpose(1, 0, 2).reshape(8, -1)
    b1f = small[:, 8:].reshape(1, -1)
    args = (x, vec, b1f, wqkv, wproj, wfc1, wfc2, dy)
    step = pair_step(n_dp, *args) if pairs else whole_mesh_step(n_fsdp, *args)
    out, dx, gwqkv, gwproj, gw1, gw2, gs = step
    return (
        out,
        dx,
        gs[0],
        gs[1],
        gwqkv,
        gs[2],
        gs[3],
        gwproj,
        gs[4],
        gs[5],
        gs[6],
        gw1,
        gs[8],
        gw2,
        gs[7],
    )


def solution(mesh):
    n_dp, n_fsdp = mesh.shape["dp"], mesh.shape["fsdp"]
    act = P(("dp", "fsdp"), None, None)
    vec = P("fsdp")
    mat = P("fsdp", None)
    in_specs = (act, vec, vec, mat, vec, vec, mat, vec, vec, vec, mat, vec, mat, vec, act)
    out_specs = (act,) + in_specs[:1] + in_specs[1:14]
    return jax.shard_map(
        lambda *a: body(n_dp, n_fsdp, *a),
        mesh=mesh,
        in_specs=in_specs,
        out_specs=out_specs,
        check_vma=False,
    )
```
